32 devices in a mesh: groups: 2 (over x), seq: 16 (over z, y, core).
Axes of the slice: x: 2, y: 2, z: 4, core: 2. Of those that a mesh axis runs over, the one named last changes fastest.
Arguments:
- activations: bfloat16 [4096, 8192], P(('groups', 'seq')), parts along dimension 0, may hold values from -6 to 6
- gate_values: bfloat16 [2, 4096, 8192], P(None, ('groups', 'seq')), parts along dimension 1, may hold values from -6 to 6
- accepted: int32 [4096], P(('groups', 'seq')), parts along dimension 0, may hold values 0 or 1
- seg_starts: int32 [4096], P(('groups', 'seq')), parts along dimension 0, may hold values from 0 to 1984, as said below
- mr_taps: bfloat16 [512, 128], replicated, may hold values from -0.5 to 0.5
- lr_rate: float32 [512, 16], replicated, as said below
- lr_angle: float32 [512, 16], replicated, may hold values from -3.140625 to 3.140625
- lr_residue: float32 [2, 512, 16], replicated, may hold values from -5 to 5
Outputs:
- result: bfloat16 [4096, 8192], P(('groups', 'seq')), parts along dimension 0
The draws below stay inside these ranges and needn't reach their ends.
There are 2 independent parts, one for each index of `groups`. The reference program is written for one: setup_inputs(seed, part) draws one part's arguments, and reference() takes and returns one part's arrays. A program takes and returns all parts, laid end to end along the dimension named above; an argument that names none is the same for every part. Nothing has to cross between parts.
Inputs may be any that keep to these rules, and one draw needn't show every extreme that they name: seg_starts[t] is the first position of the draft segment that holds t: never falling, at most t, equal to t where a segment begins, at most 4 segments. `lr_rate`: every rate is positive.
All inputs are finite; a program needn't handle non-finite values. No bound on the sum of `accepted` on one device may be relied on, other than what follows from the above.
Results may differ from the reference program's by a relative error of at most 0.0061.
Values may be sent and summed in bfloat16 or wider, within the bound.
A program may use at most 192 MiB of HBM per device.

```python
import math
import jax
import jax.numpy as jnp
from jax import lax

D = 8192
FILTERS = 512
MODES = 16
TAPS = 128
TOK_DEV = 128
SEQ = 2048


def draw_seg_starts(key, part):
    last_cut = SEQ - TOK_DEV // 2
    random_cuts = jax.random.randint(key, (2,), 1, last_cut + 1, dtype=jnp.int32)
    cut_points = jnp.concatenate([random_cuts, jnp.full((1,), last_cut, jnp.int32)], axis=0)
    position = jnp.arange(SEQ, dtype=jnp.int32)
    chosen = jnp.where(cut_points[:, None] <= position[None, :], cut_points[:, None], 0)
    return jnp.max(chosen, axis=0).astype(jnp.int32)


def draw_lr_rate(key, part):
    key_pick, key_slow, key_fast = jax.random.split(key, 3)
    slow_share = 0.5
    low_rate = 0.2 / SEQ
    high_rate = 2.0 / SEQ
    fast_low = min(0.5 / TOK_DEV, 1.0 / 64.0)
    fast_high = 1.0 / 25.0
    chooser = jax.random.uniform(key_pick, (FILTERS, MODES), jnp.float32)
    slow_rates = jnp.exp(jax.random.uniform(key_slow, (FILTERS, MODES), jnp.float32, math.log(low_rate), math.log(high_rate)))
    fast_rates = jnp.exp(jax.random.uniform(key_fast, (FILTERS, MODES), jnp.float32, math.log(fast_low), math.log(fast_high)))
    return jnp.where(chooser < slow_share, slow_rates, fast_rates).astype(jnp.float32)


def touch_ends(result, own_key, smallest, largest):
    dims = result.shape
    index_at = [jax.random.randint(jax.random.fold_in(own_key, axis), (), 0, dims[axis]) for axis in range(len(dims))]
    result = result.at[tuple(index_at)].set(smallest)
    longest = dims.index(max(dims))
    index_at[longest] = (index_at[longest] + 1) % dims[longest]
    return result.at[tuple(index_at)].set(largest)


def level_of(rng, dims, shards, least, largest):
    def one(dim, shards_of):
        draws = jax.random.uniform(jax.random.fold_in(jax.random.fold_in(rng, 6), dim), (shards_of,), jnp.float32, least / len(shards), largest / len(shards))
        return jnp.repeat(jnp.exp(draws), dims[dim] // shards_of).reshape((-1,) + (1,) * (len(dims) - dim - 1))

    gain = one(*shards[0])
    for cut in shards[1:]:
        gain = gain * one(*cut)
    return gain


def gaussian(own_key, shape, deviation, bound, cuts=(), held_as=jnp.bfloat16):
    entries = deviation * jax.random.normal(own_key, shape, jnp.float32)
    if cuts:
        entries = entries * level_of(own_key, shape, cuts, -0.22, 0.18)
    return jnp.clip(entries, -bound, bound).astype(held_as)


def setup_inputs(seed: int = 0, part: int = 0) -> dict:
    seeds = jax.random.split(jax.random.key(seed), 9)
    part_splits = jax.random.split(jax.random.fold_in(seeds[8], part), 9)
    activations = gaussian(part_splits[0], (SEQ, D), 1.0, 6.0, ((0, 16),))
    gate_values = gaussian(part_splits[1], (2, SEQ, D), 1.0, 6.0, ((1, 16),))
    accepted = touch_ends((jax.random.randint(part_splits[2], (SEQ,), 0, 4) < 3).astype(jnp.int32), jax.random.fold_in(part_splits[2], 1), 0, 1)
    seg_starts = draw_seg_starts(jax.random.fold_in(jax.random.fold_in(seeds[8], part), 71), part)
    mr_taps = gaussian(seeds[4], (FILTERS, TAPS), TAPS ** -0.5, 0.5)
    lr_rate = draw_lr_rate(jax.random.fold_in(seeds[8], 71), part)
    lr_angle = jnp.clip(jax.random.uniform(seeds[6], (FILTERS, MODES), jnp.float32, -3.140625, 3.140625), -3.140625, 3.140625)
    lr_residue = gaussian(seeds[7], (2, FILTERS, MODES), 1.0, 5.0, (), jnp.float32)
    return {"activations": activations, "gate_values": gate_values, "accepted": accepted, "seg_starts": seg_starts, "mr_taps": mr_taps, "lr_rate": lr_rate, "lr_angle": lr_angle, "lr_residue": lr_residue}


highest = lax.Precision.HIGHEST

def lag_onehot(row_count, col_count, offset, lag_count):
    row_idx = jnp.arange(row_count, dtype=jnp.int32)[:, None, None]
    col_idx = jnp.arange(col_count, dtype=jnp.int32)[None, :, None]
    lag_idx = jnp.arange(lag_count, dtype=jnp.int32)[None, None, :]
    return (row_idx + offset - col_idx == lag_idx).astype(jnp.float32)

def lr_tables(lr_rate, lr_angle, lr_residue, length):
    lag_steps = jnp.arange(length, dtype=jnp.float32)
    rate_col = lr_rate[:, :, None]
    angle_col = lr_angle[:, :, None]
    magnitude = jnp.exp(-rate_col * lag_steps)
    pow_re = magnitude * jnp.cos(angle_col * lag_steps)
    pow_im = magnitude * jnp.sin(angle_col * lag_steps)
    res_scale = 0.25 * jnp.sqrt(lr_rate)
    res_re = (res_scale * lr_residue[0])[:, :, None]
    res_im = (res_scale * lr_residue[1])[:, :, None]
    filter_taps = lax.optimization_barrier(jnp.sum(res_re * pow_re - res_im * pow_im, axis=1)).astype(jnp.bfloat16)
    end_re = pow_re[:, :, ::-1]
    end_im = pow_im[:, :, ::-1]
    lag_next = lag_steps + 1.0
    mag_next = jnp.exp(-rate_col * lag_next)
    one_re = mag_next * jnp.cos(angle_col * lag_next)
    one_im = mag_next * jnp.sin(angle_col * lag_next)
    in_re = res_re * one_re - res_im * one_im
    in_im = res_re * one_im + res_im * one_re
    full_mag = jnp.exp(-lr_rate * length)
    full_re = full_mag * jnp.cos(lr_angle * length)
    full_im = full_mag * jnp.sin(lr_angle * length)
    return (filter_taps, end_re, end_im, in_re, in_im, full_re, full_im)

def lr_local(mid_blocks, row_starts, block_begins, tables, toeplitz):
    length = mid_blocks.shape[1]
    positions = block_begins[:, None] + jnp.arange(length, dtype=jnp.int32)[None, :]
    mid_float = mid_blocks.astype(jnp.float32)
    keep = (positions[:, None, :] >= row_starts[:, :, None]).astype(jnp.float32)
    masked_toep = toeplitz.astype(jnp.float32)[None] * keep[:, None]
    within = jnp.einsum('bgtj,bjgc->btgc', masked_toep, mid_float, precision=highest)
    last_start = row_starts[:, -1]
    keep_rows = (positions >= last_start[:, None]).astype(jnp.float32)
    kept = mid_float * keep_rows[:, :, None, None]
    b_re = jnp.einsum('gmj,bjgc->bgmc', tables[1], kept, precision=highest)
    b_im = jnp.einsum('gmj,bjgc->bgmc', tables[2], kept, precision=highest)
    carry_on = (last_start < block_begins).astype(jnp.float32)[:, None, None]
    a_re = tables[5][None] * carry_on
    a_im = tables[6][None] * carry_on
    inside = (row_starts < block_begins[:, None]).astype(jnp.float32)
    return (within, (a_re, a_im, b_re, b_im), inside)

def incoming(state_re, state_im, in_re, in_im, inside):
    added = jnp.einsum('gmt,bgmc->btgc', in_re, state_re, precision=highest)
    added = added - jnp.einsum('gmt,bgmc->btgc', in_im, state_im, precision=highest)
    return added * inside[:, :, None, None]

def reference(activations, gate_values, accepted, seg_starts, mr_taps, lr_rate, lr_angle, lr_residue):
    tok_rows = TOK_DEV
    rim_rows = TAPS - 1
    channels = D // FILTERS
    win_rows = tok_rows + rim_rows
    masked_input = activations * accepted[:, None].astype(jnp.bfloat16)
    padded = jnp.concatenate([jnp.zeros((rim_rows, D), jnp.bfloat16), masked_input], axis=0)
    onehot = lag_onehot(tok_rows, win_rows, rim_rows, TAPS)
    mr_toeplitz = jnp.einsum('tsk,gk->gts', onehot, mr_taps.astype(jnp.float32), precision=highest).astype(jnp.bfloat16)
    tables = lr_tables(lr_rate, lr_angle, lr_residue, tok_rows)
    lr_toeplitz = jnp.einsum('tjk,gk->gtj', lag_onehot(tok_rows, tok_rows, 0, tok_rows), tables[0].astype(jnp.float32), precision=highest).astype(jnp.bfloat16)

    def advance(carried, block_index):
        block_start = block_index * tok_rows
        window = lax.dynamic_slice_in_dim(padded, block_start, win_rows, 0)
        row_starts = lax.dynamic_slice_in_dim(seg_starts, block_start, tok_rows, 0)
        gate_mr = lax.dynamic_slice_in_dim(gate_values[0], block_start, tok_rows, 0)
        gate_lr = lax.dynamic_slice_in_dim(gate_values[1], block_start, tok_rows, 0)
        col_pos = block_start - rim_rows + jnp.arange(win_rows, dtype=jnp.int32)
        same_segment = (col_pos[None, :] >= row_starts[:, None]).astype(jnp.bfloat16)
        masked_toep = (mr_toeplitz * same_segment[None]).astype(jnp.float32)
        window_float = window.reshape(win_rows, FILTERS, channels).astype(jnp.float32)
        mr_out = jnp.einsum('gts,sgc->tgc', masked_toep, window_float, precision=highest).reshape(tok_rows, D)
        mid_out = (gate_mr.astype(jnp.float32) * mr_out).astype(jnp.bfloat16)
        begins = jnp.reshape(block_start, (1,)).astype(jnp.int32)
        within, summary, inside = lr_local(mid_out.reshape(1, tok_rows, FILTERS, channels), row_starts[None], begins, tables, lr_toeplitz)
        lr_out = within + incoming(carried[0][None], carried[1][None], tables[3], tables[4], inside)
        a_re, a_im, b_re, b_im = summary
        next_re = a_re[0][:, :, None] * carried[0] - a_im[0][:, :, None] * carried[1] + b_re[0]
        next_im = a_re[0][:, :, None] * carried[1] + a_im[0][:, :, None] * carried[0] + b_im[0]
        lr_round = lax.optimization_barrier(lr_out.reshape(tok_rows, D).astype(jnp.bfloat16))
        block_out = (gate_lr.astype(jnp.float32) * lr_round.astype(jnp.float32)).astype(jnp.bfloat16)
        return ((next_re, next_im), block_out)
    initial = (jnp.zeros((FILTERS, MODES, channels), jnp.float32), jnp.zeros((FILTERS, MODES, channels), jnp.float32))
    final_state, blocks = lax.scan(advance, initial, jnp.arange(SEQ // tok_rows, dtype=jnp.int32))
    return blocks.reshape(SEQ, D)
```

```python
import functools
import jax
import jax.numpy as jnp
from jax import lax
from jax.experimental import pallas as pl
from jax.experimental.pallas import tpu as pltpu
from jax.sharding import PartitionSpec as P

f32 = jnp.float32
bf16 = jnp.bfloat16
MESH = pl.DeviceIdType.MESH
LANES = 128
TEAM = 4
CHUNKS = 8


def iota(shape, dim):
    return lax.broadcasted_iota(jnp.int32, shape, dim)


def powers(lam_re, lam_im, exps):
    out_re = jnp.ones(exps.shape, f32)
    out_im = jnp.zeros(exps.shape, f32)
    base_re, base_im = lam_re, lam_im
    for bit in range(7):
        on = ((exps >> bit) & 1) == 1
        new_re = out_re * base_re - out_im * base_im
        new_im = out_re * base_im + out_im * base_re
        out_re = jnp.where(on, new_re, out_re)
        out_im = jnp.where(on, new_im, out_im)
        base_re, base_im = base_re * base_re - base_im * base_im, 2.0 * base_re * base_im
    return out_re, out_im


def squared(re, im, times):
    for _ in range(times):
        re, im = re * re - im * im, 2.0 * re * im
    return re, im


def outer(a_re, a_im, b_re, b_im, flip):
    res, ims = [], []
    for a in range(8):
        row = 7 - a if flip else a
        pr, pi = a_re[row : row + 1], a_im[row : row + 1]
        res.append(pr * b_re - pi * b_im)
        ims.append(pr * b_im + pi * b_re)
    return jnp.concatenate(res, 0), jnp.concatenate(ims, 0)


def circulant(row):
    wide = jnp.broadcast_to(row, (LANES, LANES))
    return pltpu.roll(wide, 1, 1, stride=1, stride_axis=0).astype(bf16)


def build_taps(taps, ma, mb, toep):
    for g in range(8):
        c = circulant(taps[g : g + 1, :])
        toep[g * 128 : (g + 1) * 128, :128] = c * ma[...]
        toep[g * 128 : (g + 1) * 128, 128:] = c * mb[...]


def build_tables(lam):
    lam_re, lam_im, res_re, res_im = lam[0:1], lam[1:2], lam[2:3], lam[3:4]
    a_re, a_im = powers(lam_re, lam_im, iota((8, LANES), 0) * 16)
    p_re, p_im = powers(lam_re, lam_im, 15 - iota((16, LANES), 0))
    end_re, end_im = outer(a_re, a_im, p_re, p_im, True)
    real = res_re * end_re - res_im * end_im
    high = real.astype(bf16)
    low = (real - high.astype(f32)).astype(bf16)
    pick = (iota((8, LANES), 1) // 16 == iota((8, LANES), 0)).astype(bf16)
    near = lax.dot_general(jnp.concatenate([pick, pick], 1), jnp.concatenate([high, low], 1),
                           (((1,), (1,)), ((), ())), preferred_element_type=f32)
    return end_re.astype(bf16), end_im.astype(bf16), near.astype(bf16).astype(f32)


def mid_dot(prev, cur, gate, toep):
    full = jnp.dot(toep[...], jnp.concatenate([prev, cur], axis=0), preferred_element_type=f32)
    group = iota((128, LANES), 1) // 16
    mr = full[:128]
    for g in range(1, 8):
        mr = jnp.where(group == g, full[g * 128 : (g + 1) * 128], mr)
    return (gate.astype(f32) * mr).astype(bf16)


def ends_dot(mid, keep, end_re, end_im):
    kept = mid * keep[...]
    group16 = iota((16, LANES), 1) // 16
    parts = []
    for table in (end_re, end_im):
        whole = lax.dot_general(table, kept, (((0,), (0,)), ((), ())), preferred_element_type=f32)
        got = whole[:16]
        for g in range(1, 8):
            got = jnp.where(group16 == g, whole[g * 16 : (g + 1) * 16], got)
        parts.append(got)
    return jnp.concatenate(parts, 0).astype(bf16)


def near_tile(mid, near, mb, toep):
    for g in range(8):
        c = circulant(near[g : g + 1, :])
        half = (g % 2) * 128
        row = (g // 2) * 128
        toep[row : row + 128, half : half + 128] = c * mb[...]
    group = iota((128, LANES), 1) // 16
    even = (group % 2 == 0).astype(bf16)
    window = jnp.concatenate([mid * even, mid * (1 - even)], axis=0)
    full = jnp.dot(toep[:512, :], window, preferred_element_type=f32)
    lr = full[:128]
    for g in range(1, 4):
        lr = jnp.where(group // 2 == g, full[g * 128 : (g + 1) * 128], lr)
    return lr


def far_tile(lr, state, lam, gate, inside):
    lam_re, lam_im, res_re, res_im = lam[0:1], lam[1:2], lam[2:3], lam[3:4]
    a_re, a_im = powers(lam_re, lam_im, iota((8, LANES), 0) * 16)
    p_re, p_im = powers(lam_re, lam_im, 1 + iota((16, LANES), 0))
    q_re = res_re * p_re - res_im * p_im
    q_im = res_re * p_im + res_im * p_re
    in_re, in_im = outer(a_re, a_im, q_re, q_im, False)
    table = jnp.concatenate([in_re.astype(bf16) * inside[...], (-in_im).astype(bf16) * inside[...]], 1)
    group16 = iota((16, LANES), 1) // 16
    spread = []
    for ri in range(2):
        for g in range(8):
            spread.append(state[ri * 16 : (ri + 1) * 16, :] * (group16 == g).astype(bf16))
    lr = lr + jnp.dot(table, jnp.concatenate(spread, 0), preferred_element_type=f32)
    return (gate.astype(f32) * lr.astype(bf16).astype(f32)).astype(bf16)


def kernel(n, unroll, act_hbm, gates_hbm, acc, seg, taps, rate, angle, resid, out,
           act, gates, halo, mid, near, lr, back, lam, groups, lam_end, toep,
           ma, mb_mr, mb_lr, keep, inside, meta, metas, prev_meta, tflag, tflags,
           bbuf, brecv, lbuf, lrecv, pbuf, land,
           in_sem, hs, hr, ms, mr, ns, nr, ts, tr, bs, br, ls, lrs, ps, pr):
    rows, width = act.shape
    teams = n // TEAM
    span = width // CHUNKS
    quarter = span // TEAM
    tiles = span // LANES
    per_owner = tiles // TEAM
    me = lax.axis_index("seq")
    team = me // TEAM
    rank = lax.rem(me, TEAM)

    def looped(lo, hi, fn):
        def run(i, _):
            fn(i)
            return 0
        lax.fori_loop(lo, hi, run, 0)

    def mate(k):
        return team * TEAM + lax.rem(rank + k, TEAM)

    def peer(k):
        return lax.rem(me + k * TEAM, n)

    nxt, prv = lax.rem(me + 1, n), lax.rem(me + n - 1, n)
    barrier = pltpu.get_barrier_semaphore()

    def greet(to):
        pl.semaphore_signal(barrier, inc=1, device_id={"seq": to}, device_id_type=MESH)

    looped(1, TEAM, lambda k: greet(mate(k)))
    looped(1, teams, lambda k: greet(peer(k)))

    @pl.when(rank == TEAM - 1)
    def _():
        greet(nxt)

    @pl.when(rank == 0)
    def _():
        greet(prv)

    def lanes_of(c):
        return pl.ds(pl.multiple_of(c * span, LANES), span)

    def load(c, i):
        if i == 0:
            return pltpu.make_async_copy(act_hbm.at[:, lanes_of(c)], act.at[:, lanes_of(c)], in_sem.at[0, c])
        return pltpu.make_async_copy(gates_hbm.at[i - 1, :, lanes_of(c)], gates.at[i - 1, :, lanes_of(c)],
                                     in_sem.at[i, c])

    def load_two(c):
        load(c, 0).start()
        load(c, 1).start()

    looped(0, CHUNKS, load_two)
    looped(0, CHUNKS, lambda c: load(c, 2).start())

    def remote(src, dst, send, recv_sem, to):
        return pltpu.make_async_remote_copy(src_ref=src, dst_ref=dst, send_sem=send, recv_sem=recv_sem,
                                            device_id={"seq": to}, device_id_type=MESH)

    def halo_copy(c):
        return remote(act_hbm.at[:, lanes_of(c)], halo.at[:, lanes_of(c)], hs.at[c], hr.at[c], nxt)

    def next_meta():
        return remote(meta, prev_meta, ns.at[0], nr.at[0], nxt)

    def meta_copy(k):
        return remote(meta, metas.at[rank], ms.at[k], mr.at[k], mate(k))

    def tflag_copy(k):
        return remote(tflag, tflags.at[team], ts.at[k], tr.at[k], peer(k))

    def b_copy(c, k):
        return remote(bbuf.at[c, lax.rem(rank + k, TEAM)], brecv.at[c, rank], bs.at[c, k], br.at[c, k], mate(k))

    def l_copy(c, k):
        return remote(lbuf.at[c], lrecv.at[c, team], ls.at[c, k], lrs.at[c, k], peer(k))

    def p_copy(c, k):
        return remote(pbuf.at[c, lax.rem(rank + k, TEAM)], land.at[c, rank], ps.at[c, k], pr.at[c, k], mate(k))

    first = jnp.transpose(jnp.broadcast_to((seg[...] - me * rows).astype(f32), (LANES, LANES)))
    last = first[LANES - 1 : LANES, :]
    t = iota((LANES, LANES), 0)
    j = iota((LANES, LANES), 1)
    tf, jf = t.astype(f32), j.astype(f32)
    own = acc[...].astype(f32)
    meta[:8] = jnp.broadcast_to(own, (8, LANES))
    meta[8:] = jnp.broadcast_to((last < 0).astype(f32), (8, LANES))

    pl.semaphore_wait(barrier, TEAM - 1 + teams - 1 + (rank == 0).astype(jnp.int32)
                      + (rank == TEAM - 1).astype(jnp.int32))

    @pl.when(me < n - 1)
    def _():
        next_meta().start()
        looped(0, CHUNKS, lambda c: halo_copy(c).start())

    looped(1, TEAM, lambda k: meta_copy(k).start())

    within = ((j <= t) & (jf >= first)).astype(f32)
    mb_lr[...] = within.astype(bf16)
    mb_mr[...] = (within * own).astype(bf16)
    keep[...] = (tf >= last).astype(f32).astype(bf16)
    inside[...] = (first < 0).astype(f32).astype(bf16)

    flip = (iota((LANES, LANES), 0) + iota((LANES, LANES), 1) == LANES - 1).astype(bf16)
    back[...] = jnp.dot(taps[...], flip, preferred_element_type=f32)
    mag = jnp.exp(-rate[...])
    scale = 0.25 * jnp.sqrt(rate[...])
    lam_re, lam_im = mag * jnp.cos(angle[...]), mag * jnp.sin(angle[...])
    groups[0] = lam_re
    groups[1] = lam_im
    groups[2] = scale * resid[0]
    groups[3] = scale * resid[1]
    end_re, end_im = squared(lam_re, lam_im, 7)
    lam_end[:16] = end_re
    lam_end[16:] = end_im
    group_lane = iota((16, LANES), 1) // 16
    diagonal = iota((16, LANES), 0) == lax.rem(iota((16, LANES), 1), 16)

    def pick_lanes(x, idx):
        return jnp.take_along_axis(x, idx, axis=1, mode="promise_in_bounds")

    for block in range(groups.shape[2] // LANES):
        def spread_lam(k):
            idx = group_lane + 8 * k
            got = []
            for i in range(4):
                x = pick_lanes(groups[i, :, block * LANES : (block + 1) * LANES], idx)
                got.append(jnp.sum(jnp.where(diagonal, x, 0.0), axis=0, keepdims=True))
            got.append(jnp.zeros((4, LANES), f32))
            at = pl.ds(pl.multiple_of((block * 16 + k) * 8, 8), 8)
            lam[at, :] = jnp.concatenate(got, 0)
        looped(0, 16, spread_lam)

    looped(1, TEAM, lambda k: meta_copy(k).wait())
    metas[rank] = meta[...]
    whole = metas[0, 8:]
    for i in range(1, TEAM):
        whole = whole * metas[i, 8:]
    tflag[...] = whole

    def later(k, fn):
        @pl.when(team + k < teams)
        def _():
            fn()

    def earlier(k, fn):
        @pl.when(team >= k)
        def _():
            fn()

    looped(1, teams, lambda k: later(k, lambda: tflag_copy(k).start()))

    @pl.when(me > 0)
    def _():
        next_meta().wait_recv()
        ma[...] = (((j > t) & (jf - rows >= first)).astype(f32) * prev_meta[0:1, :]).astype(bf16)

    @pl.when(me == 0)
    def _():
        ma[...] = jnp.zeros_like(ma)
        halo[...] = jnp.zeros_like(halo)

    looped(1, teams, lambda k: earlier(k, lambda: tflag_copy(k).wait_recv()))

    def owner_decay(c):
        res = []
        for i in range(per_owner):
            tile = c * tiles + rank * per_owner + i
            block = tile // 16
            x = lam_end[:, pl.ds(pl.multiple_of(block * LANES, LANES), LANES)]
            idx = iota((32, LANES), 1) // 16 + 8 * lax.rem(tile, 16)
            res.append(pick_lanes(x, idx))
        d = jnp.concatenate(res, 1)
        return d[:16], d[16:]

    def advance(state, a_re, a_im, go, piece):
        s_re, s_im = state
        piece = piece.astype(f32)
        f_re, f_im = a_re * go, a_im * go
        return f_re * s_re - f_im * s_im + piece[:16], f_re * s_im + f_im * s_re + piece[16:]

    def where_of(c, i):
        where = []
        for u in range(unroll):
            k = i * unroll + u
            tile = c * tiles + k
            where.append((pl.ds(pl.multiple_of(tile * LANES, LANES), LANES),
                          pl.ds(pl.multiple_of(tile * 8, 8), 8),
                          k // per_owner,
                          pl.ds(pl.multiple_of(lax.rem(k, per_owner) * LANES, LANES), LANES)))
        return where

    def first_part(c):
        load(c, 0).wait()
        load(c, 1).wait()

        @pl.when(me > 0)
        def _():
            halo_copy(c).wait_recv()

        def group(i):
            where = where_of(c, i)
            for u, (lanes, eight, owner, local) in enumerate(where):
                build_taps(back[eight, :], ma, mb_mr, toep.at[u])
            tables = [build_tables(lam[eight, :]) for lanes, eight, owner, local in where]
            mids = [mid_dot(halo[:, lanes], act[:, lanes], gates[0, :, lanes], toep.at[u])
                    for u, (lanes, eight, owner, local) in enumerate(where)]
            ends = [ends_dot(m, keep, tb[0], tb[1]) for m, tb in zip(mids, tables)]
            for (lanes, eight, owner, local), m, b, tb in zip(where, mids, ends, tables):
                mid[:, lanes] = m
                bbuf[c, owner, :, local] = b
                near[eight, :] = tb[2]

        looped(0, tiles // unroll, group)
        looped(1, TEAM, lambda k: b_copy(c, k).start())
        brecv[c, rank] = bbuf[c, rank]

    def combine(c):
        looped(1, TEAM, lambda k: b_copy(c, k).wait_recv())
        a_re, a_im = owner_decay(c)
        state = jnp.zeros((16, quarter), f32), jnp.zeros((16, quarter), f32)
        for i in range(TEAM):
            state = advance(state, a_re, a_im, metas[i, 8:9, 0:1], brecv[c, i])
        lbuf[c, :16] = state[0].astype(bf16)
        lbuf[c, 16:] = state[1].astype(bf16)
        looped(1, teams, lambda k: later(k, lambda: l_copy(c, k).start()))

    def spread(c):
        looped(1, teams, lambda k: earlier(k, lambda: l_copy(c, k).wait_recv()))
        a_re, a_im = owner_decay(c)
        t_re, t_im = squared(a_re, a_im, TEAM.bit_length() - 1)

        def step(i, state):
            return advance(state, t_re, t_im, tflags[i][0:1, 0:1], lrecv[c, i])

        zero = jnp.zeros((16, quarter), f32)
        state = lax.fori_loop(0, team, step, (zero, zero))
        for i in range(TEAM):
            pbuf[c, i, :16] = state[0].astype(bf16)
            pbuf[c, i, 16:] = state[1].astype(bf16)
            if i < TEAM - 1:
                state = advance(state, a_re, a_im, metas[i, 8:9, 0:1], brecv[c, i])
        looped(1, TEAM, lambda k: p_copy(c, k).start())
        land[c, rank] = pbuf[c, rank]

    def second(c):
        def group(i):
            for u, (lanes, eight, owner, local) in enumerate(where_of(c, i)):
                lr[:, lanes] = near_tile(mid[:, lanes], near[eight, :], mb_lr, toep.at[u])
        looped(0, tiles // unroll, group)

    def third(c):
        load(c, 2).wait()
        looped(1, TEAM, lambda k: p_copy(c, k).wait_recv())

        def group(i):
            for u, (lanes, eight, owner, local) in enumerate(where_of(c, i)):
                out[:, lanes] = far_tile(lr[:, lanes], land[c, owner, :, local], lam[eight, :],
                                         gates[1, :, lanes], inside)
        looped(0, tiles // unroll, group)

    def step_all(s):
        def at(lag, fn):
            @pl.when((s >= lag) & (s < CHUNKS + lag))
            def _():
                fn(s - lag)
        at(0, first_part)
        at(2, second)
        at(1, combine)
        at(2, spread)
        at(3, third)

    looped(0, CHUNKS + 3, step_all)

    @pl.when(me < n - 1)
    def _():
        next_meta().wait_send()
        looped(0, CHUNKS, lambda c: halo_copy(c).wait_send())

    looped(1, teams, lambda k: later(k, lambda: tflag_copy(k).wait_send()))

    def drain(c):
        looped(1, TEAM, lambda k: b_copy(c, k).wait_send())
        looped(1, TEAM, lambda k: p_copy(c, k).wait_send())
        looped(1, teams, lambda k: later(k, lambda: l_copy(c, k).wait_send()))

    looped(0, CHUNKS, drain)


def shards(activations, gate_values, accepted, seg_starts, mr_taps, lr_rate, lr_angle, lr_residue):
    rows, width = activations.shape
    count, taps = mr_taps.shape
    modes = lr_rate.shape[1]
    n = lax.axis_size("seq")
    teams = n // TEAM
    span = width // CHUNKS
    quarter = span // TEAM
    tiles = span // LANES
    unroll = 4 if tiles % 4 == 0 else 1
    both = 2 * modes

    def dma(*shape):
        return pltpu.SemaphoreType.DMA(shape)

    vmem = pl.BlockSpec(memory_space=pltpu.VMEM)
    hbm = pl.BlockSpec(memory_space=pltpu.HBM)
    mask = pltpu.VMEM((rows, LANES), bf16)
    return pl.pallas_call(
        functools.partial(kernel, n, unroll),
        in_specs=[hbm] * 2 + [vmem] * 6,
        out_specs=vmem,
        out_shape=jax.ShapeDtypeStruct((rows, width), bf16),
        scratch_shapes=[
            pltpu.VMEM((rows, width), bf16), pltpu.VMEM((2, rows, width), bf16),
            pltpu.VMEM((rows, width), bf16), pltpu.VMEM((rows, width), bf16),
            pltpu.VMEM((count, taps), f32), pltpu.VMEM((rows, width), f32),
            pltpu.VMEM((count, taps), f32), pltpu.VMEM((width // LANES * 8, LANES), f32),
            pltpu.VMEM((4, modes, count), f32), pltpu.VMEM((both, count), f32),
            pltpu.VMEM((unroll, 8 * rows, 2 * rows), bf16),
            mask, mask, mask, mask, mask,
            pltpu.VMEM((16, LANES), f32), pltpu.VMEM((TEAM, 16, LANES), f32), pltpu.VMEM((16, LANES), f32),
            pltpu.VMEM((8, LANES), f32), pltpu.VMEM((teams, 8, LANES), f32),
            pltpu.VMEM((CHUNKS, TEAM, both, quarter), bf16), pltpu.VMEM((CHUNKS, TEAM, both, quarter), bf16),
            pltpu.VMEM((CHUNKS, both, quarter), bf16), pltpu.VMEM((CHUNKS, teams, both, quarter), bf16),
            pltpu.VMEM((CHUNKS, TEAM, both, quarter), bf16), pltpu.VMEM((CHUNKS, TEAM, both, quarter), bf16),
            dma(3, CHUNKS), dma(CHUNKS), dma(CHUNKS), dma(TEAM), dma(TEAM), dma(1), dma(1), dma(teams), dma(teams),
            dma(CHUNKS, TEAM), dma(CHUNKS, TEAM), dma(CHUNKS, teams), dma(CHUNKS, teams),
            dma(CHUNKS, TEAM), dma(CHUNKS, TEAM)],
        compiler_params=pltpu.CompilerParams(collective_id=0, has_side_effects=True,
                                             vmem_limit_bytes=54 * 2**20),
        name="hyena",
    )(activations, gate_values, accepted[None, :], seg_starts[None, :], mr_taps, lr_rate.T, lr_angle.T,
      jnp.swapaxes(lr_residue, 1, 2))


def solution(mesh):
    return jax.shard_map(
        shards,
        mesh=mesh,
        in_specs=(P(("groups", "seq"), None), P(None, ("groups", "seq"), None), P(("groups", "seq")),
                  P(("groups", "seq")), P(), P(), P(), P()),
        out_specs=P(("groups", "seq"), None),
        check_vma=False,
    )
```

```python
import functools
import jax
import jax.numpy as jnp
from jax import lax
from jax.experimental import pallas as pl
from jax.experimental.pallas import tpu as pltpu
from jax.sharding import PartitionSpec as P

f32 = jnp.float32
bf16 = jnp.bfloat16
MESH = pl.DeviceIdType.MESH
LANES = 128
TEAM = 4
CHUNKS = 8
AHEAD = 2


def iota(shape, dim):
    return lax.broadcasted_iota(jnp.int32, shape, dim)


def powers(lam_re, lam_im, exps):
    out_re = jnp.ones(exps.shape, f32)
    out_im = jnp.zeros(exps.shape, f32)
    base_re, base_im = lam_re, lam_im
    for bit in range(7):
        on = ((exps >> bit) & 1) == 1
        new_re = out_re * base_re - out_im * base_im
        new_im = out_re * base_im + out_im * base_re
        out_re = jnp.where(on, new_re, out_re)
        out_im = jnp.where(on, new_im, out_im)
        base_re, base_im = base_re * base_re - base_im * base_im, 2.0 * base_re * base_im
    return out_re, out_im


def squared(re, im, times):
    for _ in range(times):
        re, im = re * re - im * im, 2.0 * re * im
    return re, im


def outer(a_re, a_im, b_re, b_im, flip):
    res, ims = [], []
    for a in range(8):
        row = 7 - a if flip else a
        pr, pi = a_re[row : row + 1], a_im[row : row + 1]
        res.append(pr * b_re - pi * b_im)
        ims.append(pr * b_im + pi * b_re)
    return jnp.concatenate(res, 0), jnp.concatenate(ims, 0)


def circulant(row):
    wide = jnp.broadcast_to(row, (LANES, LANES))
    return pltpu.roll(wide, 1, 1, stride=1, stride_axis=0).astype(bf16)


def build_taps(taps, ma, mb, toep):
    for g in range(8):
        c = circulant(taps[g : g + 1, :])
        toep[g * 128 : (g + 1) * 128, :128] = c * ma[...]
        toep[g * 128 : (g + 1) * 128, 128:] = c * mb[...]


def build_tables(lam):
    lam_re, lam_im, res_re, res_im = lam[0:1], lam[1:2], lam[2:3], lam[3:4]
    a_re, a_im = powers(lam_re, lam_im, iota((8, LANES), 0) * 16)
    p_re, p_im = powers(lam_re, lam_im, 15 - iota((16, LANES), 0))
    end_re, end_im = outer(a_re, a_im, p_re, p_im, True)
    real = res_re * end_re - res_im * end_im
    high = real.astype(bf16)
    low = (real - high.astype(f32)).astype(bf16)
    pick = (iota((8, LANES), 1) // 16 == iota((8, LANES), 0)).astype(bf16)
    near = lax.dot_general(jnp.concatenate([pick, pick], 1), jnp.concatenate([high, low], 1),
                           (((1,), (1,)), ((), ())), preferred_element_type=f32)
    return end_re.astype(bf16), end_im.astype(bf16), near.astype(bf16).astype(f32)


def mid_dot(prev, cur, gate, toep):
    full = jnp.dot(toep[...], jnp.concatenate([prev, cur], axis=0), preferred_element_type=f32)
    group = iota((128, LANES), 1) // 16
    mr = full[:128]
    for g in range(1, 8):
        mr = jnp.where(group == g, full[g * 128 : (g + 1) * 128], mr)
    return (gate.astype(f32) * mr).astype(bf16)


def ends_dot(mid, keep, end_re, end_im):
    kept = mid * keep[...]
    group16 = iota((16, LANES), 1) // 16
    parts = []
    for table in (end_re, end_im):
        whole = lax.dot_general(table, kept, (((0,), (0,)), ((), ())), preferred_element_type=f32)
        got = whole[:16]
        for g in range(1, 8):
            got = jnp.where(group16 == g, whole[g * 16 : (g + 1) * 16], got)
        parts.append(got)
    return jnp.concatenate(parts, 0).astype(bf16)


def near_tile(mid, near, mb, toep):
    for g in range(8):
        c = circulant(near[g : g + 1, :])
        half = (g % 2) * 128
        row = (g // 2) * 128
        toep[row : row + 128, half : half + 128] = c * mb[...]
    group = iota((128, LANES), 1) // 16
    even = (group % 2 == 0).astype(bf16)
    window = jnp.concatenate([mid * even, mid * (1 - even)], axis=0)
    full = jnp.dot(toep[:512, :], window, preferred_element_type=f32)
    lr = full[:128]
    for g in range(1, 4):
        lr = jnp.where(group // 2 == g, full[g * 128 : (g + 1) * 128], lr)
    return lr


def far_tile(lr, state, lam, gate, inside):
    lam_re, lam_im, res_re, res_im = lam[0:1], lam[1:2], lam[2:3], lam[3:4]
    a_re, a_im = powers(lam_re, lam_im, iota((8, LANES), 0) * 16)
    p_re, p_im = powers(lam_re, lam_im, 1 + iota((16, LANES), 0))
    q_re = res_re * p_re - res_im * p_im
    q_im = res_re * p_im + res_im * p_re
    in_re, in_im = outer(a_re, a_im, q_re, q_im, False)
    table = jnp.concatenate([in_re.astype(bf16) * inside[...], (-in_im).astype(bf16) * inside[...]], 1)
    group16 = iota((16, LANES), 1) // 16
    spread = []
    for ri in range(2):
        for g in range(8):
            spread.append(state[ri * 16 : (ri + 1) * 16, :] * (group16 == g).astype(bf16))
    lr = lr + jnp.dot(table, jnp.concatenate(spread, 0), preferred_element_type=f32)
    return (gate.astype(f32) * lr.astype(bf16).astype(f32)).astype(bf16)


def kernel(n, unroll, act_hbm, gates_hbm, acc, seg, taps, rate, angle, resid, out,
           act, gates, halo, mid, near, lr, back, lam, groups, lam_end, toep,
           ma, mb_mr, mb_lr, keep, inside, meta, metas, prev_meta, tflag, tflags,
           bbuf, brecv, lbuf, lrecv, pbuf, land,
           in_sem, hs, hr, ms, mr, ns, nr, ts, tr, bs, br, ls, lrs, ps, pr):
    rows, width = act.shape
    teams = n // TEAM
    span = width // CHUNKS
    quarter = span // TEAM
    tiles = span // LANES
    per_owner = tiles // TEAM
    me = lax.axis_index("seq")
    team = me // TEAM
    rank = lax.rem(me, TEAM)

    def looped(lo, hi, fn):
        def run(i, _):
            fn(i)
            return 0
        lax.fori_loop(lo, hi, run, 0)

    def mate(k):
        return team * TEAM + lax.rem(rank + k, TEAM)

    def peer(k):
        return lax.rem(me + k * TEAM, n)

    nxt, prv = lax.rem(me + 1, n), lax.rem(me + n - 1, n)
    barrier = pltpu.get_barrier_semaphore()

    def greet(to):
        pl.semaphore_signal(barrier, inc=1, device_id={"seq": to}, device_id_type=MESH)

    looped(1, TEAM, lambda k: greet(mate(k)))
    looped(1, teams, lambda k: greet(peer(k)))

    @pl.when(rank == TEAM - 1)
    def _():
        greet(nxt)

    @pl.when(rank == 0)
    def _():
        greet(prv)

    def lanes_of(c):
        return pl.ds(pl.multiple_of(c * span, LANES), span)

    def load(c, i):
        if i == 0:
            return pltpu.make_async_copy(act_hbm.at[:, lanes_of(c)], act.at[:, lanes_of(c)], in_sem.at[0, c])
        return pltpu.make_async_copy(gates_hbm.at[i - 1, :, lanes_of(c)], gates.at[i - 1, :, lanes_of(c)],
                                     in_sem.at[i, c])

    looped(0, CHUNKS, lambda c: load(c, 0).start())
    looped(0, CHUNKS, lambda c: load(c, 1).start())
    looped(0, CHUNKS, lambda c: load(c, 2).start())

    def remote(src, dst, send, recv_sem, to):
        return pltpu.make_async_remote_copy(src_ref=src, dst_ref=dst, send_sem=send, recv_sem=recv_sem,
                                            device_id={"seq": to}, device_id_type=MESH)

    def halo_copy(c):
        return remote(act.at[:, lanes_of(c)], halo.at[:, lanes_of(c)], hs.at[c], hr.at[c], nxt)

    def next_meta():
        return remote(meta, prev_meta, ns.at[0], nr.at[0], nxt)

    def meta_copy(k):
        return remote(meta, metas.at[rank], ms.at[k], mr.at[k], mate(k))

    def tflag_copy(k):
        return remote(tflag, tflags.at[team], ts.at[k], tr.at[k], peer(k))

    def b_copy(c, k):
        return remote(bbuf.at[c, lax.rem(rank + k, TEAM)], brecv.at[c, rank], bs.at[c, k], br.at[c, k], mate(k))

    def l_copy(c, k):
        return remote(lbuf.at[c], lrecv.at[c, team], ls.at[c, k], lrs.at[c, k], peer(k))

    def p_copy(c, k):
        return remote(pbuf.at[c, lax.rem(rank + k, TEAM)], land.at[c, rank], ps.at[c, k], pr.at[c, k], mate(k))

    first = jnp.transpose(jnp.broadcast_to((seg[...] - me * rows).astype(f32), (LANES, LANES)))
    last = first[LANES - 1 : LANES, :]
    t = iota((LANES, LANES), 0)
    j = iota((LANES, LANES), 1)
    tf, jf = t.astype(f32), j.astype(f32)
    own = acc[...].astype(f32)
    meta[:8] = jnp.broadcast_to(own, (8, LANES))
    meta[8:] = jnp.broadcast_to((last < 0).astype(f32), (8, LANES))

    pl.semaphore_wait(barrier, TEAM - 1 + teams - 1 + (rank == 0).astype(jnp.int32)
                      + (rank == TEAM - 1).astype(jnp.int32))

    @pl.when(me < n - 1)
    def _():
        next_meta().start()

    def send_halo(c):
        load(c, 0).wait()

        @pl.when(me < n - 1)
        def _():
            halo_copy(c).start()

    looped(0, AHEAD, send_halo)

    looped(1, TEAM, lambda k: meta_copy(k).start())

    within = ((j <= t) & (jf >= first)).astype(f32)
    mb_lr[...] = within.astype(bf16)
    mb_mr[...] = (within * own).astype(bf16)
    keep[...] = (tf >= last).astype(f32).astype(bf16)
    inside[...] = (first < 0).astype(f32).astype(bf16)

    flip = (iota((LANES, LANES), 0) + iota((LANES, LANES), 1) == LANES - 1).astype(bf16)
    back[...] = jnp.dot(taps[...], flip, preferred_element_type=f32)
    mag = jnp.exp(-rate[...])
    scale = 0.25 * jnp.sqrt(rate[...])
    lam_re, lam_im = mag * jnp.cos(angle[...]), mag * jnp.sin(angle[...])
    groups[0] = lam_re
    groups[1] = lam_im
    groups[2] = scale * resid[0]
    groups[3] = scale * resid[1]
    end_re, end_im = squared(lam_re, lam_im, 7)
    lam_end[:16] = end_re
    lam_end[16:] = end_im
    group_lane = iota((16, LANES), 1) // 16
    diagonal = iota((16, LANES), 0) == lax.rem(iota((16, LANES), 1), 16)

    def pick_lanes(x, idx):
        return jnp.take_along_axis(x, idx, axis=1, mode="promise_in_bounds")

    for block in range(groups.shape[2] // LANES):
        def spread_lam(k):
            idx = group_lane + 8 * k
            got = []
            for i in range(4):
                x = pick_lanes(groups[i, :, block * LANES : (block + 1) * LANES], idx)
                got.append(jnp.sum(jnp.where(diagonal, x, 0.0), axis=0, keepdims=True))
            got.append(jnp.zeros((4, LANES), f32))
            at = pl.ds(pl.multiple_of((block * 16 + k) * 8, 8), 8)
            lam[at, :] = jnp.concatenate(got, 0)
        looped(0, 16, spread_lam)

    looped(1, TEAM, lambda k: meta_copy(k).wait())
    metas[rank] = meta[...]
    whole = metas[0, 8:]
    for i in range(1, TEAM):
        whole = whole * metas[i, 8:]
    tflag[...] = whole

    def later(k, fn):
        @pl.when(team + k < teams)
        def _():
            fn()

    def earlier(k, fn):
        @pl.when(team >= k)
        def _():
            fn()

    looped(1, teams, lambda k: later(k, lambda: tflag_copy(k).start()))

    @pl.when(me > 0)
    def _():
        next_meta().wait_recv()
        ma[...] = (((j > t) & (jf - rows >= first)).astype(f32) * prev_meta[0:1, :]).astype(bf16)

    @pl.when(me == 0)
    def _():
        ma[...] = jnp.zeros_like(ma)
        halo[...] = jnp.zeros_like(halo)

    looped(1, teams, lambda k: earlier(k, lambda: tflag_copy(k).wait_recv()))

    def owner_decay(c):
        res = []
        for i in range(per_owner):
            tile = c * tiles + rank * per_owner + i
            block = tile // 16
            x = lam_end[:, pl.ds(pl.multiple_of(block * LANES, LANES), LANES)]
            idx = iota((32, LANES), 1) // 16 + 8 * lax.rem(tile, 16)
            res.append(pick_lanes(x, idx))
        d = jnp.concatenate(res, 1)
        return d[:16], d[16:]

    def advance(state, a_re, a_im, go, piece):
        s_re, s_im = state
        piece = piece.astype(f32)
        f_re, f_im = a_re * go, a_im * go
        return f_re * s_re - f_im * s_im + piece[:16], f_re * s_im + f_im * s_re + piece[16:]

    def where_of(c, i):
        where = []
        for u in range(unroll):
            k = i * unroll + u
            tile = c * tiles + k
            where.append((pl.ds(pl.multiple_of(tile * LANES, LANES), LANES),
                          pl.ds(pl.multiple_of(tile * 8, 8), 8),
                          k // per_owner,
                          pl.ds(pl.multiple_of(lax.rem(k, per_owner) * LANES, LANES), LANES)))
        return where

    def first_part(c):
        load(c, 1).wait()

        @pl.when(me > 0)
        def _():
            halo_copy(c).wait_recv()

        @pl.when(c + AHEAD < CHUNKS)
        def _():
            @pl.when(me < n - 1)
            def _():
                halo_copy(c).wait_send()

            send_halo(c + AHEAD)

        def group(i):
            where = where_of(c, i)
            for u, (lanes, eight, owner, local) in enumerate(where):
                build_taps(back[eight, :], ma, mb_mr, toep.at[u])
            tables = [build_tables(lam[eight, :]) for lanes, eight, owner, local in where]
            mids = [mid_dot(halo[:, lanes], act[:, lanes], gates[0, :, lanes], toep.at[u])
                    for u, (lanes, eight, owner, local) in enumerate(where)]
            ends = [ends_dot(m, keep, tb[0], tb[1]) for m, tb in zip(mids, tables)]
            for (lanes, eight, owner, local), m, b, tb in zip(where, mids, ends, tables):
                mid[:, lanes] = m
                bbuf[c, owner, :, local] = b
                near[eight, :] = tb[2]

        looped(0, tiles // unroll, group)
        looped(1, TEAM, lambda k: b_copy(c, k).start())
        brecv[c, rank] = bbuf[c, rank]

    def combine(c):
        looped(1, TEAM, lambda k: b_copy(c, k).wait_recv())
        a_re, a_im = owner_decay(c)
        state = jnp.zeros((16, quarter), f32), jnp.zeros((16, quarter), f32)
        for i in range(TEAM):
            state = advance(state, a_re, a_im, metas[i, 8:9, 0:1], brecv[c, i])
        lbuf[c, :16] = state[0].astype(bf16)
        lbuf[c, 16:] = state[1].astype(bf16)
        looped(1, teams, lambda k: later(k, lambda: l_copy(c, k).start()))

    def spread(c):
        looped(1, teams, lambda k: earlier(k, lambda: l_copy(c, k).wait_recv()))
        a_re, a_im = owner_decay(c)
        t_re, t_im = squared(a_re, a_im, TEAM.bit_length() - 1)

        def step(i, state):
            return advance(state, t_re, t_im, tflags[i][0:1, 0:1], lrecv[c, i])

        zero = jnp.zeros((16, quarter), f32)
        state = lax.fori_loop(0, team, step, (zero, zero))
        for i in range(TEAM):
            pbuf[c, i, :16] = state[0].astype(bf16)
            pbuf[c, i, 16:] = state[1].astype(bf16)
            if i < TEAM - 1:
                state = advance(state, a_re, a_im, metas[i, 8:9, 0:1], brecv[c, i])
        looped(1, TEAM, lambda k: p_copy(c, k).start())
        land[c, rank] = pbuf[c, rank]

    def second(c):
        def group(i):
            for u, (lanes, eight, owner, local) in enumerate(where_of(c, i)):
                lr[:, lanes] = near_tile(mid[:, lanes], near[eight, :], mb_lr, toep.at[u])
        looped(0, tiles // unroll, group)

    def third(c):
        load(c, 2).wait()
        looped(1, TEAM, lambda k: p_copy(c, k).wait_recv())

        def group(i):
            for u, (lanes, eight, owner, local) in enumerate(where_of(c, i)):
                out[:, lanes] = far_tile(lr[:, lanes], land[c, owner, :, local], lam[eight, :],
                                         gates[1, :, lanes], inside)
        looped(0, tiles // unroll, group)

    def step_all(s):
        def at(lag, fn):
            @pl.when((s >= lag) & (s < CHUNKS + lag))
            def _():
                fn(s - lag)
        at(0, first_part)
        at(2, second)
        at(1, combine)
        at(2, spread)
        at(3, third)

    looped(0, CHUNKS + 3, step_all)

    @pl.when(me < n - 1)
    def _():
        next_meta().wait_send()
        looped(CHUNKS - AHEAD, CHUNKS, lambda c: halo_copy(c).wait_send())

    looped(1, teams, lambda k: later(k, lambda: tflag_copy(k).wait_send()))

    def drain(c):
        looped(1, TEAM, lambda k: b_copy(c, k).wait_send())
        looped(1, TEAM, lambda k: p_copy(c, k).wait_send())
        looped(1, teams, lambda k: later(k, lambda: l_copy(c, k).wait_send()))

    looped(0, CHUNKS, drain)


def shards(activations, gate_values, accepted, seg_starts, mr_taps, lr_rate, lr_angle, lr_residue):
    rows, width = activations.shape
    count, taps = mr_taps.shape
    modes = lr_rate.shape[1]
    n = lax.axis_size("seq")
    teams = n // TEAM
    span = width // CHUNKS
    quarter = span // TEAM
    tiles = span // LANES
    unroll = 4 if tiles % 4 == 0 else 1
    both = 2 * modes

    def dma(*shape):
        return pltpu.SemaphoreType.DMA(shape)

    vmem = pl.BlockSpec(memory_space=pltpu.VMEM)
    hbm = pl.BlockSpec(memory_space=pltpu.HBM)
    mask = pltpu.VMEM((rows, LANES), bf16)
    return pl.pallas_call(
        functools.partial(kernel, n, unroll),
        in_specs=[hbm] * 2 + [vmem] * 6,
        out_specs=vmem,
        out_shape=jax.ShapeDtypeStruct((rows, width), bf16),
        scratch_shapes=[
            pltpu.VMEM((rows, width), bf16), pltpu.VMEM((2, rows, width), bf16),
            pltpu.VMEM((rows, width), bf16), pltpu.VMEM((rows, width), bf16),
            pltpu.VMEM((count, taps), f32), pltpu.VMEM((rows, width), f32),
            pltpu.VMEM((count, taps), f32), pltpu.VMEM((width // LANES * 8, LANES), f32),
            pltpu.VMEM((4, modes, count), f32), pltpu.VMEM((both, count), f32),
            pltpu.VMEM((unroll, 8 * rows, 2 * rows), bf16),
            mask, mask, mask, mask, mask,
            pltpu.VMEM((16, LANES), f32), pltpu.VMEM((TEAM, 16, LANES), f32), pltpu.VMEM((16, LANES), f32),
            pltpu.VMEM((8, LANES), f32), pltpu.VMEM((teams, 8, LANES), f32),
            pltpu.VMEM((CHUNKS, TEAM, both, quarter), bf16), pltpu.VMEM((CHUNKS, TEAM, both, quarter), bf16),
            pltpu.VMEM((CHUNKS, both, quarter), bf16), pltpu.VMEM((CHUNKS, teams, both, quarter), bf16),
            pltpu.VMEM((CHUNKS, TEAM, both, quarter), bf16), pltpu.VMEM((CHUNKS, TEAM, both, quarter), bf16),
            dma(3, CHUNKS), dma(CHUNKS), dma(CHUNKS), dma(TEAM), dma(TEAM), dma(1), dma(1), dma(teams), dma(teams),
            dma(CHUNKS, TEAM), dma(CHUNKS, TEAM), dma(CHUNKS, teams), dma(CHUNKS, teams),
            dma(CHUNKS, TEAM), dma(CHUNKS, TEAM)],
        compiler_params=pltpu.CompilerParams(collective_id=0, has_side_effects=True,
                                             vmem_limit_bytes=50 * 2**20),
        name="hyena",
    )(activations, gate_values, accepted[None, :], seg_starts[None, :], mr_taps, lr_rate.T, lr_angle.T,
      jnp.swapaxes(lr_residue, 1, 2))


def solution(mesh):
    return jax.shard_map(
        shards,
        mesh=mesh,
        in_specs=(P(("groups", "seq"), None), P(None, ("groups", "seq"), None), P(("groups", "seq")),
                  P(("groups", "seq")), P(), P(), P(), P()),
        out_specs=P(("groups", "seq"), None),
        check_vma=False,
    )
```

```python
import functools
import jax
import jax.numpy as jnp
from jax import lax
from jax.experimental import pallas as pl
from jax.experimental.pallas import tpu as pltpu
from jax.sharding import PartitionSpec as P

f32 = jnp.float32
bf16 = jnp.bfloat16
MESH = pl.DeviceIdType.MESH
LANES = 128
TEAM = 4
CHUNKS = 8
NEAR_LAG = 2
OWN_LAG = 2


def iota(shape, dim):
    return lax.broadcasted_iota(jnp.int32, shape, dim)


def powers(re, im, exps, bits):
    on = (exps & 1) == 1
    out_re, out_im = jnp.where(on, re, 1.0), jnp.where(on, im, 0.0)
    for bit in range(1, bits):
        re, im = re * re - im * im, 2.0 * re * im
        on = ((exps >> bit) & 1) == 1
        new_re = out_re * re - out_im * im
        new_im = out_re * im + out_im * re
        out_re = jnp.where(on, new_re, out_re)
        out_im = jnp.where(on, new_im, out_im)
    return out_re, out_im


def squared(re, im, times):
    for _ in range(times):
        re, im = re * re - im * im, 2.0 * re * im
    return re, im


def outer(a_re, a_im, b_re, b_im, flip):
    res, ims = [], []
    for a in range(8):
        row = 7 - a if flip else a
        pr, pi = a_re[row : row + 1], a_im[row : row + 1]
        res.append(pr * b_re - pi * b_im)
        ims.append(pr * b_im + pi * b_re)
    return jnp.concatenate(res, 0), jnp.concatenate(ims, 0)


def circulant(row):
    wide = jnp.broadcast_to(row, (LANES, LANES))
    return pltpu.roll(wide, 1, 1, stride=1, stride_axis=0).astype(bf16)


def build_taps(taps, ma, mb, toep):
    for g in range(8):
        c = circulant(taps[g : g + 1, :])
        toep[g * 128 : (g + 1) * 128, :128] = c * ma[...]
        toep[g * 128 : (g + 1) * 128, 128:] = c * mb[...]


def build_tables(lam):
    lam_re, lam_im, res_re, res_im = lam[0:1], lam[1:2], lam[2:3], lam[3:4]
    a_re, a_im = powers(*squared(lam_re, lam_im, 4), iota((8, LANES), 0), 3)
    p_re, p_im = powers(lam_re, lam_im, 15 - iota((16, LANES), 0), 4)
    end_re, end_im = outer(a_re, a_im, p_re, p_im, True)
    real = res_re * end_re - res_im * end_im
    high = real.astype(bf16)
    low = (real - high.astype(f32)).astype(bf16)
    pick = (iota((8, LANES), 1) // 16 == iota((8, LANES), 0)).astype(bf16)
    near = lax.dot_general(jnp.concatenate([pick, pick], 1), jnp.concatenate([high, low], 1),
                           (((1,), (1,)), ((), ())), preferred_element_type=f32)
    return end_re.astype(bf16), end_im.astype(bf16), near.astype(bf16).astype(f32)


def mid_dot(prev, cur, gate, toep):
    full = jnp.dot(toep[...], jnp.concatenate([prev, cur], axis=0), preferred_element_type=f32)
    group = iota((128, LANES), 1) // 16
    mr = full[:128]
    for g in range(1, 8):
        mr = jnp.where(group == g, full[g * 128 : (g + 1) * 128], mr)
    return (gate.astype(f32) * mr).astype(bf16)


def ends_dot(mid, keep, end_re, end_im):
    kept = mid * keep[...]
    group16 = iota((16, LANES), 1) // 16
    parts = []
    for table in (end_re, end_im):
        whole = lax.dot_general(table, kept, (((0,), (0,)), ((), ())), preferred_element_type=f32)
        got = whole[:16]
        for g in range(1, 8):
            got = jnp.where(group16 == g, whole[g * 16 : (g + 1) * 16], got)
        parts.append(got)
    return jnp.concatenate(parts, 0).astype(bf16)


def build_near(near, mb, toep):
    for g in range(8):
        c = circulant(near[g : g + 1, :])
        half = (g % 2) * 128
        row = (g // 2) * 128
        toep[row : row + 128, half : half + 128] = c * mb[...]


def near_dot(mid, toep):
    group = iota((128, LANES), 1) // 16
    even = (group % 2 == 0).astype(bf16)
    window = jnp.concatenate([mid * even, mid * (1 - even)], axis=0)
    full = jnp.dot(toep[...], window, preferred_element_type=f32)
    lr = full[:128]
    for g in range(1, 4):
        lr = jnp.where(group // 2 == g, full[g * 128 : (g + 1) * 128], lr)
    return lr


def far_tile(lr, state, lam, gate, inside):
    lam_re, lam_im, res_re, res_im = lam[0:1], lam[1:2], lam[2:3], lam[3:4]
    a_re, a_im = powers(*squared(lam_re, lam_im, 4), iota((8, LANES), 0), 3)
    p_re, p_im = powers(lam_re, lam_im, iota((16, LANES), 0), 4)
    res_re, res_im = res_re * lam_re - res_im * lam_im, res_re * lam_im + res_im * lam_re
    q_re = res_re * p_re - res_im * p_im
    q_im = res_re * p_im + res_im * p_re
    in_re, in_im = outer(a_re, a_im, q_re, q_im, False)
    table = jnp.concatenate([in_re.astype(bf16) * inside[...], (-in_im).astype(bf16) * inside[...]], 1)
    group16 = iota((16, LANES), 1) // 16
    spread = []
    for ri in range(2):
        for g in range(8):
            spread.append(state[ri * 16 : (ri + 1) * 16, :] * (group16 == g).astype(bf16))
    lr = lr + jnp.dot(table, jnp.concatenate(spread, 0), preferred_element_type=f32)
    return (gate.astype(f32) * lr.astype(bf16).astype(f32)).astype(bf16)


def kernel(n, act_hbm, gates_hbm, acc, seg, taps, rate, angle, resid, out,
           act, gates, halo, mid, near, lr, back, lam, groups, lam_end, toep, toep_near,
           ma, mb_mr, mb_lr, keep, inside, meta, metas, prev_meta, tflag, tflags,
           bbuf, brecv, lbuf, lrecv, pbuf, land,
           result, in_sem, out_sem, hs, hr, ms, mr, ns, nr, ts, tr, bs, br, ls, lrs, ps, pr):
    rows, width = act.shape
    teams = n // TEAM
    span = width // CHUNKS
    quarter = span // TEAM
    tiles = span // LANES
    per_owner = tiles // TEAM
    me = lax.axis_index("seq")
    team = me // TEAM
    rank = lax.rem(me, TEAM)

    def looped(lo, hi, fn):
        def run(i, _):
            fn(i)
            return 0
        lax.fori_loop(lo, hi, run, 0)

    def mate(k):
        return team * TEAM + lax.rem(rank + k, TEAM)

    def peer(k):
        return lax.rem(me + k * TEAM, n)

    nxt, prv = lax.rem(me + 1, n), lax.rem(me + n - 1, n)
    barrier = pltpu.get_barrier_semaphore()

    def greet(to):
        pl.semaphore_signal(barrier, inc=1, device_id={"seq": to}, device_id_type=MESH)

    looped(1, TEAM, lambda k: greet(mate(k)))
    looped(1, teams, lambda k: greet(peer(k)))

    @pl.when(rank == TEAM - 1)
    def _():
        greet(nxt)

    @pl.when(rank == 0)
    def _():
        greet(prv)

    def lanes_of(c):
        return pl.ds(pl.multiple_of(c * span, LANES), span)

    def load(c, i):
        if i == 0:
            return pltpu.make_async_copy(act_hbm.at[:, lanes_of(c)], act.at[:, lanes_of(c)], in_sem.at[0, c])
        return pltpu.make_async_copy(gates_hbm.at[i - 1, :, lanes_of(c)], gates.at[i - 1, :, lanes_of(c)],
                                     in_sem.at[i, c])

    looped(0, CHUNKS, lambda c: load(c, 0).start())
    looped(0, CHUNKS, lambda c: load(c, 1).start())
    looped(0, CHUNKS, lambda c: load(c, 2).start())

    def remote(src, dst, send, recv_sem, to):
        return pltpu.make_async_remote_copy(src_ref=src, dst_ref=dst, send_sem=send, recv_sem=recv_sem,
                                            device_id={"seq": to}, device_id_type=MESH)

    def halo_copy(c):
        return remote(act.at[:, lanes_of(c)], halo.at[:, lanes_of(c)], hs.at[c], hr.at[c], nxt)

    def next_meta():
        return remote(meta, prev_meta, ns.at[0], nr.at[0], nxt)

    def meta_copy(k):
        return remote(meta, metas.at[rank], ms.at[k], mr.at[k], mate(k))

    def tflag_copy(k):
        return remote(tflag, tflags.at[team], ts.at[k], tr.at[k], peer(k))

    def b_copy(c, k):
        return remote(bbuf.at[c, lax.rem(rank + k, TEAM)], brecv.at[c, rank], bs.at[c, k], br.at[c, k], mate(k))

    def l_copy(c, k):
        return remote(lbuf.at[c], lrecv.at[c, team], ls.at[c, k], lrs.at[c, k], peer(k))

    def p_copy(c, k):
        return remote(pbuf.at[c, lax.rem(rank + k, TEAM)], land.at[c, rank], ps.at[c, k], pr.at[c, k], mate(k))

    first = jnp.transpose(jnp.broadcast_to((seg[...] - me * rows).astype(f32), (LANES, LANES)))
    last = first[LANES - 1 : LANES, :]
    t = iota((LANES, LANES), 0)
    j = iota((LANES, LANES), 1)
    tf, jf = t.astype(f32), j.astype(f32)
    own = acc[...].astype(f32)
    meta[:8] = jnp.broadcast_to(own, (8, LANES))
    meta[8:] = jnp.broadcast_to((last < 0).astype(f32), (8, LANES))

    pl.semaphore_wait(barrier, TEAM - 1 + teams - 1 + (rank == 0).astype(jnp.int32)
                      + (rank == TEAM - 1).astype(jnp.int32))

    @pl.when(me < n - 1)
    def _():
        next_meta().start()

    def send_halo(c):
        load(c, 0).wait()

        @pl.when(me < n - 1)
        def _():
            halo_copy(c).start()

    send_halo(0)

    looped(1, TEAM, lambda k: meta_copy(k).start())

    within = ((j <= t) & (jf >= first)).astype(f32)
    mb_lr[...] = within.astype(bf16)
    mb_mr[...] = (within * own).astype(bf16)
    keep[...] = (tf >= last).astype(f32).astype(bf16)
    inside[...] = (first < 0).astype(f32).astype(bf16)

    flip = (iota((LANES, LANES), 0) + iota((LANES, LANES), 1) == LANES - 1).astype(bf16)
    back[...] = jnp.dot(taps[...], flip, preferred_element_type=f32)
    mag = jnp.exp(-rate[...])
    scale = 0.25 * jnp.sqrt(rate[...])
    lam_re, lam_im = mag * jnp.cos(angle[...]), mag * jnp.sin(angle[...])
    groups[0] = lam_re
    groups[1] = lam_im
    groups[2] = scale * resid[0]
    groups[3] = scale * resid[1]
    end_re, end_im = squared(lam_re, lam_im, 7)
    lam_end[:16] = end_re
    lam_end[16:] = end_im
    group_lane = iota((16, LANES), 1) // 16
    diagonal = iota((16, LANES), 0) == lax.rem(iota((16, LANES), 1), 16)

    def pick_lanes(x, idx):
        return jnp.take_along_axis(x, idx, axis=1, mode="promise_in_bounds")

    blocks = groups.shape[2] // LANES

    def spread_lam(k):
        idx = group_lane + 8 * k
        picked = [[pick_lanes(groups[i, :, block * LANES : (block + 1) * LANES], idx) for i in range(4)]
                  for block in range(blocks)]
        for block in range(blocks):
            got = [jnp.sum(jnp.where(diagonal, x, 0.0), axis=0, keepdims=True) for x in picked[block]]
            got.append(jnp.zeros((4, LANES), f32))
            at = pl.ds(pl.multiple_of((block * 16 + k) * 8, 8), 8)
            lam[at, :] = jnp.concatenate(got, 0)

    looped(0, 16, spread_lam)

    @pl.when(me < n - 1)
    def _():
        halo_copy(0).wait_send()

    send_halo(1)

    looped(1, TEAM, lambda k: meta_copy(k).wait())
    metas[rank] = meta[...]
    whole = metas[0, 8:]
    for i in range(1, TEAM):
        whole = whole * metas[i, 8:]
    tflag[...] = whole

    def later(k, fn):
        @pl.when(team + k < teams)
        def _():
            fn()

    def earlier(k, fn):
        @pl.when(team >= k)
        def _():
            fn()

    looped(1, teams, lambda k: later(k, lambda: tflag_copy(k).start()))

    @pl.when(me > 0)
    def _():
        next_meta().wait_recv()
        ma[...] = (((j > t) & (jf - rows >= first)).astype(f32) * prev_meta[0:1, :]).astype(bf16)

    @pl.when(me == 0)
    def _():
        ma[...] = jnp.zeros_like(ma)
        halo[...] = jnp.zeros_like(halo)

    looped(1, teams, lambda k: earlier(k, lambda: tflag_copy(k).wait_recv()))

    def owner_decay(c):
        res = []
        for i in range(per_owner):
            tile = c * tiles + rank * per_owner + i
            block = tile // 16
            x = lam_end[:, pl.ds(pl.multiple_of(block * LANES, LANES), LANES)]
            idx = iota((32, LANES), 1) // 16 + 8 * lax.rem(tile, 16)
            res.append(pick_lanes(x, idx))
        d = jnp.concatenate(res, 1)
        return d[:16], d[16:]

    def advance(state, a_re, a_im, go, piece):
        s_re, s_im = state
        piece = piece.astype(f32)
        f_re, f_im = a_re * go, a_im * go
        return f_re * s_re - f_im * s_im + piece[:16], f_re * s_im + f_im * s_re + piece[16:]

    def where_of(c):
        where = []
        for k in range(tiles):
            tile = c * tiles + k
            where.append((pl.ds(pl.multiple_of(tile * LANES, LANES), LANES),
                          pl.ds(pl.multiple_of(tile * 8, 8), 8),
                          k // per_owner,
                          pl.ds(k % per_owner * LANES, LANES)))
        return where

    def work(c1, c2, c3):
        stores = []
        if c1 is not None:
            where1 = where_of(c1)
            for u, (lanes, eight, owner, local) in enumerate(where1):
                build_taps(back[eight, :], ma, mb_mr, toep.at[u])
            tables = [build_tables(lam[eight, :]) for lanes, eight, owner, local in where1]
            mids = [mid_dot(halo[:, lanes], act[:, lanes], gates[0, :, lanes], toep.at[u])
                    for u, (lanes, eight, owner, local) in enumerate(where1)]
            ends = [ends_dot(m, keep, tb[0], tb[1]) for m, tb in zip(mids, tables)]
        if c3 is not None:
            where3 = where_of(c3)
            outs = [far_tile(lr[:, lanes], land[c3, owner, :, local], lam[eight, :],
                             gates[1, :, lanes], inside) for lanes, eight, owner, local in where3]
        if c2 is not None:
            where2 = where_of(c2)
            for u, (lanes, eight, owner, local) in enumerate(where2):
                build_near(near[eight, :], mb_lr, toep_near.at[u])
            lrs = [near_dot(mid[:, lanes], toep_near.at[u])
                   for u, (lanes, eight, owner, local) in enumerate(where2)]
        if c3 is not None:
            for (lanes, eight, owner, local), o in zip(where3, outs):
                result[:, lanes] = o
        if c2 is not None:
            for (lanes, eight, owner, local), o in zip(where2, lrs):
                lr[:, lanes] = o
        if c1 is not None:
            for (lanes, eight, owner, local), m, b, tb in zip(where1, mids, ends, tables):
                mid[:, lanes] = m
                bbuf[c1, owner, :, local] = b
                near[eight, :] = tb[2]

    def ready_first(c):
        load(c, 1).wait()

        @pl.when(me > 0)
        def _():
            halo_copy(c).wait_recv()

        @pl.when((c > 0) & (me < n - 1))
        def _():
            halo_copy(c).wait_send()

        @pl.when(c + 2 < CHUNKS)
        def _():
            send_halo(c + 2)

    def store(c):
        return pltpu.make_async_copy(result.at[:, lanes_of(c)], out.at[:, lanes_of(c)], out_sem.at[c])

    def ready_third(c):
        load(c, 2).wait()
        looped(1, TEAM, lambda k: p_copy(c, k).wait_recv())

    def send_ends(c):
        looped(1, TEAM, lambda k: b_copy(c, k).start())
        brecv[c, rank] = bbuf[c, rank]

    def combine(c):
        looped(1, TEAM, lambda k: b_copy(c, k).wait_recv())
        a_re, a_im = owner_decay(c)
        state = jnp.zeros((16, quarter), f32), jnp.zeros((16, quarter), f32)
        for i in range(TEAM):
            state = advance(state, a_re, a_im, metas[i, 8:9, 0:1], brecv[c, i])
        lbuf[c, :16] = state[0].astype(bf16)
        lbuf[c, 16:] = state[1].astype(bf16)
        looped(1, teams, lambda k: later(k, lambda: l_copy(c, k).start()))

    def spread(c):
        looped(1, teams, lambda k: earlier(k, lambda: l_copy(c, k).wait_recv()))
        a_re, a_im = owner_decay(c)
        t_re, t_im = squared(a_re, a_im, TEAM.bit_length() - 1)

        def step(i, state):
            return advance(state, t_re, t_im, tflags[i][0:1, 0:1], lrecv[c, i])

        zero = jnp.zeros((16, quarter), f32)
        state = lax.fori_loop(0, team, step, (zero, zero))
        for i in range(TEAM):
            pbuf[c, i, :16] = state[0].astype(bf16)
            pbuf[c, i, 16:] = state[1].astype(bf16)
            if i < TEAM - 1:
                state = advance(state, a_re, a_im, metas[i, 8:9, 0:1], brecv[c, i])
        looped(1, TEAM, lambda k: p_copy(c, k).start())
        land[c, rank] = pbuf[c, rank]

    def step(s):
        def at(lag, fn, until=CHUNKS):
            @pl.when((s >= lag) & (s < until + lag))
            def _():
                fn(s - lag)

        def filters(c):
            ready_first(c)
            work(c, jnp.maximum(c - NEAR_LAG, 0), None)
            send_ends(c)

        def near_only(c):
            work(None, c, None)

        def far(c):
            ready_third(c)
            work(None, None, c)
            store(c).start()

        at(0, filters)

        @pl.when((s >= CHUNKS) & (s < CHUNKS + NEAR_LAG))
        def _():
            near_only(s - NEAR_LAG)

        at(OWN_LAG, combine)
        at(2 * OWN_LAG, spread)
        at(3 * OWN_LAG, far)

    looped(0, CHUNKS + 3 * OWN_LAG, step)
    looped(0, CHUNKS, lambda c: store(c).wait())

    @pl.when(me < n - 1)
    def _():
        next_meta().wait_send()

    looped(1, teams, lambda k: later(k, lambda: tflag_copy(k).wait_send()))

    def drain(c):
        looped(1, TEAM, lambda k: b_copy(c, k).wait_send())
        looped(1, TEAM, lambda k: p_copy(c, k).wait_send())
        looped(1, teams, lambda k: later(k, lambda: l_copy(c, k).wait_send()))

    looped(0, CHUNKS, drain)


def shards(activations, gate_values, accepted, seg_starts, mr_taps, lr_rate, lr_angle, lr_residue):
    rows, width = activations.shape
    count, taps = mr_taps.shape
    modes = lr_rate.shape[1]
    n = lax.axis_size("seq")
    teams = n // TEAM
    span = width // CHUNKS
    quarter = span // TEAM
    tiles = span // LANES
    both = 2 * modes

    def dma(*shape):
        return pltpu.SemaphoreType.DMA(shape)

    vmem = pl.BlockSpec(memory_space=pltpu.VMEM)
    hbm = pl.BlockSpec(memory_space=pltpu.HBM)
    mask = pltpu.VMEM((rows, LANES), bf16)
    return pl.pallas_call(
        functools.partial(kernel, n),
        in_specs=[hbm] * 2 + [vmem] * 6,
        out_specs=hbm,
        out_shape=jax.ShapeDtypeStruct((rows, width), bf16),
        scratch_shapes=[
            pltpu.VMEM((rows, width), bf16), pltpu.VMEM((2, rows, width), bf16),
            pltpu.VMEM((rows, width), bf16), pltpu.VMEM((rows, width), bf16),
            pltpu.VMEM((count, taps), f32), pltpu.VMEM((rows, width), f32),
            pltpu.VMEM((count, taps), f32), pltpu.VMEM((width // LANES * 8, LANES), f32),
            pltpu.VMEM((4, modes, count), f32), pltpu.VMEM((both, count), f32),
            pltpu.VMEM((tiles, 8 * rows, 2 * rows), bf16), pltpu.VMEM((tiles, 4 * rows, 2 * rows), bf16),
            mask, mask, mask, mask, mask,
            pltpu.VMEM((16, LANES), f32), pltpu.VMEM((TEAM, 16, LANES), f32), pltpu.VMEM((16, LANES), f32),
            pltpu.VMEM((8, LANES), f32), pltpu.VMEM((teams, 8, LANES), f32),
            pltpu.VMEM((CHUNKS, TEAM, both, quarter), bf16), pltpu.VMEM((CHUNKS, TEAM, both, quarter), bf16),
            pltpu.VMEM((CHUNKS, both, quarter), bf16), pltpu.VMEM((CHUNKS, teams, both, quarter), bf16),
            pltpu.VMEM((CHUNKS, TEAM, both, quarter), bf16), pltpu.VMEM((CHUNKS, TEAM, both, quarter), bf16),
            pltpu.VMEM((rows, width), bf16),
            dma(3, CHUNKS), dma(CHUNKS), dma(CHUNKS), dma(CHUNKS), dma(TEAM), dma(TEAM), dma(1), dma(1), dma(teams), dma(teams),
            dma(CHUNKS, TEAM), dma(CHUNKS, TEAM), dma(CHUNKS, teams), dma(CHUNKS, teams),
            dma(CHUNKS, TEAM), dma(CHUNKS, TEAM)],
        compiler_params=pltpu.CompilerParams(collective_id=0, has_side_effects=True,
                                             vmem_limit_bytes=54 * 2**20),
        name="hyena",
    )(activations, gate_values, accepted[None, :], seg_starts[None, :], mr_taps, lr_rate.T, lr_angle.T,
      jnp.swapaxes(lr_residue, 1, 2))


def solution(mesh):
    return jax.shard_map(
        shards,
        mesh=mesh,
        in_specs=(P(("groups", "seq"), None), P(None, ("groups", "seq"), None), P(("groups", "seq")),
                  P(("groups", "seq")), P(), P(), P(), P()),
        out_specs=P(("groups", "seq"), None),
        check_vma=False,
    )
```

```python
import functools
import jax
import jax.numpy as jnp
from jax import lax
from jax.experimental import pallas as pl
from jax.experimental.pallas import tpu as pltpu
from jax.sharding import PartitionSpec as P

f32 = jnp.float32
bf16 = jnp.bfloat16
MESH = pl.DeviceIdType.MESH
LANES = 128
TEAM = 4
CHUNKS = 8
NEAR_LAG = 2
OWN_LAG = 3


def iota(shape, dim):
    return lax.broadcasted_iota(jnp.int32, shape, dim)


def powers(re, im, exps, bits):
    on = (exps & 1) == 1
    out_re, out_im = jnp.where(on, re, 1.0), jnp.where(on, im, 0.0)
    for bit in range(1, bits):
        re, im = re * re - im * im, 2.0 * re * im
        on = ((exps >> bit) & 1) == 1
        new_re = out_re * re - out_im * im
        new_im = out_re * im + out_im * re
        out_re = jnp.where(on, new_re, out_re)
        out_im = jnp.where(on, new_im, out_im)
    return out_re, out_im


def squared(re, im, times):
    for _ in range(times):
        re, im = re * re - im * im, 2.0 * re * im
    return re, im


def outer(a_re, a_im, b_re, b_im, flip):
    res, ims = [], []
    for a in range(8):
        row = 7 - a if flip else a
        pr, pi = a_re[row : row + 1], a_im[row : row + 1]
        res.append(pr * b_re - pi * b_im)
        ims.append(pr * b_im + pi * b_re)
    return jnp.concatenate(res, 0), jnp.concatenate(ims, 0)


def circulant(row):
    wide = jnp.broadcast_to(row, (LANES, LANES))
    return pltpu.roll(wide, 1, 1, stride=1, stride_axis=0).astype(bf16)


def build_taps(taps, ma, mb, toep):
    for g in range(8):
        c = circulant(taps[g : g + 1, :])
        toep[g * 128 : (g + 1) * 128, :128] = c * ma[...]
        toep[g * 128 : (g + 1) * 128, 128:] = c * mb[...]


def build_tables(lam):
    lam_re, lam_im, res_re, res_im = lam[0:1], lam[1:2], lam[2:3], lam[3:4]
    a_re, a_im = powers(*squared(lam_re, lam_im, 4), iota((8, LANES), 0), 3)
    p_re, p_im = powers(lam_re, lam_im, 15 - iota((16, LANES), 0), 4)
    end_re, end_im = outer(a_re, a_im, p_re, p_im, True)
    real = res_re * end_re - res_im * end_im
    high = real.astype(bf16)
    low = (real - high.astype(f32)).astype(bf16)
    pick = (iota((8, LANES), 1) // 16 == iota((8, LANES), 0)).astype(bf16)
    near = lax.dot_general(jnp.concatenate([pick, pick], 1), jnp.concatenate([high, low], 1),
                           (((1,), (1,)), ((), ())), preferred_element_type=f32)
    return end_re.astype(bf16), end_im.astype(bf16), near.astype(bf16).astype(f32)


def mid_dot(prev, cur, gate, toep):
    full = jnp.dot(toep[...], jnp.concatenate([prev, cur], axis=0), preferred_element_type=f32)
    group = iota((128, LANES), 1) // 16
    mr = full[:128]
    for g in range(1, 8):
        mr = jnp.where(group == g, full[g * 128 : (g + 1) * 128], mr)
    return (gate.astype(f32) * mr).astype(bf16)


def ends_dot(mid, keep, end_re, end_im):
    kept = mid * keep[...]
    group16 = iota((16, LANES), 1) // 16
    parts = []
    for table in (end_re, end_im):
        whole = lax.dot_general(table, kept, (((0,), (0,)), ((), ())), preferred_element_type=f32)
        got = whole[:16]
        for g in range(1, 8):
            got = jnp.where(group16 == g, whole[g * 16 : (g + 1) * 16], got)
        parts.append(got)
    return jnp.concatenate(parts, 0).astype(bf16)


def build_near(near, mb, toep):
    for g in range(8):
        c = circulant(near[g : g + 1, :])
        half = (g % 2) * 128
        row = (g // 2) * 128
        toep[row : row + 128, half : half + 128] = c * mb[...]


def near_dot(mid, toep):
    group = iota((128, LANES), 1) // 16
    even = (group % 2 == 0).astype(bf16)
    window = jnp.concatenate([mid * even, mid * (1 - even)], axis=0)
    full = jnp.dot(toep[...], window, preferred_element_type=f32)
    lr = full[:128]
    for g in range(1, 4):
        lr = jnp.where(group // 2 == g, full[g * 128 : (g + 1) * 128], lr)
    return lr


def far_tile(lr, state, lam, gate, inside):
    lam_re, lam_im, res_re, res_im = lam[0:1], lam[1:2], lam[2:3], lam[3:4]
    a_re, a_im = powers(*squared(lam_re, lam_im, 4), iota((8, LANES), 0), 3)
    p_re, p_im = powers(lam_re, lam_im, iota((16, LANES), 0), 4)
    res_re, res_im = res_re * lam_re - res_im * lam_im, res_re * lam_im + res_im * lam_re
    q_re = res_re * p_re - res_im * p_im
    q_im = res_re * p_im + res_im * p_re
    in_re, in_im = outer(a_re, a_im, q_re, q_im, False)
    table = jnp.concatenate([in_re.astype(bf16) * inside[...], (-in_im).astype(bf16) * inside[...]], 1)
    group16 = iota((16, LANES), 1) // 16
    spread = []
    for ri in range(2):
        for g in range(8):
            spread.append(state[ri * 16 : (ri + 1) * 16, :] * (group16 == g).astype(bf16))
    lr = lr + jnp.dot(table, jnp.concatenate(spread, 0), preferred_element_type=f32)
    return (gate.astype(f32) * lr.astype(bf16).astype(f32)).astype(bf16)


def kernel(n, act_hbm, gates_hbm, acc_hbm, seg_hbm, taps_hbm, rate_hbm, angle_hbm, resid_hbm, out,
           acc, seg, taps, rate, angle, resid, act, gates, halo, mid, near, lr, back, lam, groups, lam_end, toep, toep_near,
           ma, mb_mr, mb_lr, keep, inside, meta, metas, prev_meta, tflag, tflags,
           bbuf, brecv, lbuf, lrecv, pbuf, land,
           result, small_sem, in_sem, out_sem, hs, hr, ms, mr, ns, nr, ts, tr, bs, br, ls, lrs, ps, pr):
    rows, width = act.shape
    teams = n // TEAM
    span = width // CHUNKS
    quarter = span // TEAM
    tiles = span // LANES
    per_owner = tiles // TEAM
    me = lax.axis_index("seq")
    team = me // TEAM
    rank = lax.rem(me, TEAM)

    def looped(lo, hi, fn):
        def run(i, _):
            fn(i)
            return 0
        lax.fori_loop(lo, hi, run, 0)

    def mate(k):
        return team * TEAM + lax.rem(rank + k, TEAM)

    def peer(k):
        return lax.rem(me + k * TEAM, n)

    nxt, prv = lax.rem(me + 1, n), lax.rem(me + n - 1, n)
    barrier = pltpu.get_barrier_semaphore()

    def greet(to):
        pl.semaphore_signal(barrier, inc=1, device_id={"seq": to}, device_id_type=MESH)

    looped(1, TEAM, lambda k: greet(mate(k)))
    looped(1, teams, lambda k: greet(peer(k)))

    @pl.when(rank == TEAM - 1)
    def _():
        greet(nxt)

    @pl.when(rank == 0)
    def _():
        greet(prv)

    def lanes_of(c):
        return pl.ds(pl.multiple_of(c * span, LANES), span)

    def load(c, i):
        if i == 0:
            return pltpu.make_async_copy(act_hbm.at[:, lanes_of(c)], act.at[:, lanes_of(c)], in_sem.at[0, c])
        return pltpu.make_async_copy(gates_hbm.at[i - 1, :, lanes_of(c)], gates.at[i - 1, :, lanes_of(c)],
                                     in_sem.at[i, c])

    def fetch(i):
        src, dst = ((acc_hbm, acc), (seg_hbm, seg), (taps_hbm, taps), (rate_hbm, rate),
                    (angle_hbm, angle), (resid_hbm, resid))[i]
        return pltpu.make_async_copy(src, dst, small_sem.at[i])

    load(0, 0).start()
    for i in range(6):
        fetch(i).start()
    load(0, 1).start()
    looped(1, CHUNKS, lambda c: load(c, 0).start())
    looped(1, CHUNKS, lambda c: load(c, 1).start())
    looped(0, CHUNKS, lambda c: load(c, 2).start())

    def remote(src, dst, send, recv_sem, to):
        return pltpu.make_async_remote_copy(src_ref=src, dst_ref=dst, send_sem=send, recv_sem=recv_sem,
                                            device_id={"seq": to}, device_id_type=MESH)

    def halo_copy(c):
        return remote(act.at[:, lanes_of(c)], halo.at[:, lanes_of(c)], hs.at[c], hr.at[c], nxt)

    def next_meta():
        return remote(meta, prev_meta, ns.at[0], nr.at[0], nxt)

    def meta_copy(k):
        return remote(meta, metas.at[rank], ms.at[k], mr.at[k], mate(k))

    def tflag_copy(k):
        return remote(tflag, tflags.at[team], ts.at[k], tr.at[k], peer(k))

    def b_copy(c, k):
        return remote(bbuf.at[c, lax.rem(rank + k, TEAM)], brecv.at[c, rank], bs.at[c, k], br.at[c, k], mate(k))

    def l_copy(c, k):
        return remote(lbuf.at[c], lrecv.at[c, team], ls.at[c, k], lrs.at[c, k], peer(k))

    def p_copy(c, k):
        return remote(pbuf.at[c, lax.rem(rank + k, TEAM)], land.at[c, rank], ps.at[c, k], pr.at[c, k], mate(k))

    def send_halo(c):
        load(c, 0).wait()

        @pl.when(me < n - 1)
        def _():
            halo_copy(c).start()

    pl.semaphore_wait(barrier, TEAM - 1 + teams - 1 + (rank == 0).astype(jnp.int32)
                      + (rank == TEAM - 1).astype(jnp.int32))
    send_halo(0)

    fetch(0).wait()
    fetch(1).wait()
    first = jnp.transpose(jnp.broadcast_to((seg[...] - me * rows).astype(f32), (LANES, LANES)))
    last = first[LANES - 1 : LANES, :]
    own = acc[...].astype(f32)
    meta[:8] = jnp.broadcast_to(own, (8, LANES))
    meta[8:] = jnp.broadcast_to((last < 0).astype(f32), (8, LANES))

    @pl.when(me < n - 1)
    def _():
        next_meta().start()

    looped(1, TEAM, lambda k: meta_copy(k).start())
    t = iota((LANES, LANES), 0)
    j = iota((LANES, LANES), 1)
    tf, jf = t.astype(f32), j.astype(f32)
    within = ((j <= t) & (jf >= first)).astype(f32)
    mb_lr[...] = within.astype(bf16)
    mb_mr[...] = (within * own).astype(bf16)
    keep[...] = (tf >= last).astype(f32).astype(bf16)
    inside[...] = (first < 0).astype(f32).astype(bf16)
    prev_mask = ((j > t) & (jf - rows >= first)).astype(f32)

    for i in range(2, 6):
        fetch(i).wait()
    flip = (iota((LANES, LANES), 0) + iota((LANES, LANES), 1) == LANES - 1).astype(bf16)
    back[...] = jnp.dot(taps[...], flip, preferred_element_type=f32)
    mag = jnp.exp(-rate[...])
    scale = 0.25 * jnp.sqrt(rate[...])
    lam_re, lam_im = mag * jnp.cos(angle[...]), mag * jnp.sin(angle[...])
    groups[0] = lam_re
    groups[1] = lam_im
    groups[2] = scale * resid[0]
    groups[3] = scale * resid[1]
    end_re, end_im = squared(lam_re, lam_im, 7)
    lam_end[:16] = end_re
    lam_end[16:] = end_im
    group_lane = iota((16, LANES), 1) // 16
    diagonal = iota((16, LANES), 0) == lax.rem(iota((16, LANES), 1), 16)

    def pick_lanes(x, idx):
        return jnp.take_along_axis(x, idx, axis=1, mode="promise_in_bounds")

    blocks = groups.shape[2] // LANES

    def spread_lam(k):
        idx = group_lane + 8 * k
        picked = [[pick_lanes(groups[i, :, block * LANES : (block + 1) * LANES], idx) for i in range(4)]
                  for block in range(blocks)]
        for block in range(blocks):
            got = [jnp.sum(jnp.where(diagonal, x, 0.0), axis=0, keepdims=True) for x in picked[block]]
            got.append(jnp.zeros((4, LANES), f32))
            at = pl.ds(pl.multiple_of((block * 16 + k) * 8, 8), 8)
            lam[at, :] = jnp.concatenate(got, 0)

    looped(0, 16, spread_lam)

    @pl.when(me < n - 1)
    def _():
        halo_copy(0).wait_send()

    send_halo(1)

    @pl.when(me > 0)
    def _():
        next_meta().wait_recv()
        ma[...] = (prev_mask * prev_meta[0:1, :]).astype(bf16)

    @pl.when(me == 0)
    def _():
        ma[...] = jnp.zeros_like(ma)
        halo[...] = jnp.zeros_like(halo)

    def team_flags():
        looped(1, TEAM, lambda k: meta_copy(k).wait())
        metas[rank] = meta[...]
        whole = metas[0, 8:]
        for i in range(1, TEAM):
            whole = whole * metas[i, 8:]
        tflag[...] = whole
        looped(1, teams, lambda k: later(k, lambda: tflag_copy(k).start()))

    def later(k, fn):
        @pl.when(team + k < teams)
        def _():
            fn()

    def earlier(k, fn):
        @pl.when(team >= k)
        def _():
            fn()

    def owner_decay(c):
        res = []
        for i in range(per_owner):
            tile = c * tiles + rank * per_owner + i
            block = tile // 16
            x = lam_end[:, pl.ds(pl.multiple_of(block * LANES, LANES), LANES)]
            idx = iota((32, LANES), 1) // 16 + 8 * lax.rem(tile, 16)
            res.append(pick_lanes(x, idx))
        d = jnp.concatenate(res, 1)
        return d[:16], d[16:]

    def advance(state, a_re, a_im, go, piece):
        s_re, s_im = state
        piece = piece.astype(f32)
        f_re, f_im = a_re * go, a_im * go
        return f_re * s_re - f_im * s_im + piece[:16], f_re * s_im + f_im * s_re + piece[16:]

    def where_of(c):
        where = []
        for k in range(tiles):
            tile = c * tiles + k
            where.append((pl.ds(pl.multiple_of(tile * LANES, LANES), LANES),
                          pl.ds(pl.multiple_of(tile * 8, 8), 8),
                          k // per_owner,
                          pl.ds(k % per_owner * LANES, LANES)))
        return where

    def work(c1, c2, c3):
        stores = []
        if c1 is not None:
            where1 = where_of(c1)
            for u, (lanes, eight, owner, local) in enumerate(where1):
                build_taps(back[eight, :], ma, mb_mr, toep.at[u])
            tables = [build_tables(lam[eight, :]) for lanes, eight, owner, local in where1]
            mids = [mid_dot(halo[:, lanes], act[:, lanes], gates[0, :, lanes], toep.at[u])
                    for u, (lanes, eight, owner, local) in enumerate(where1)]
            ends = [ends_dot(m, keep, tb[0], tb[1]) for m, tb in zip(mids, tables)]
        if c3 is not None:
            where3 = where_of(c3)
            outs = [far_tile(lr[:, lanes], land[c3, owner, :, local], lam[eight, :],
                             gates[1, :, lanes], inside) for lanes, eight, owner, local in where3]
        if c2 is not None:
            where2 = where_of(c2)
            for u, (lanes, eight, owner, local) in enumerate(where2):
                build_near(near[eight, :], mb_lr, toep_near.at[u])
            lrs = [near_dot(mid[:, lanes], toep_near.at[u])
                   for u, (lanes, eight, owner, local) in enumerate(where2)]
        if c3 is not None:
            for (lanes, eight, owner, local), o in zip(where3, outs):
                result[:, lanes] = o
        if c2 is not None:
            for (lanes, eight, owner, local), o in zip(where2, lrs):
                lr[:, lanes] = o
        if c1 is not None:
            for (lanes, eight, owner, local), m, b, tb in zip(where1, mids, ends, tables):
                mid[:, lanes] = m
                bbuf[c1, owner, :, local] = b
                near[eight, :] = tb[2]

    def ready_first(c):
        load(c, 1).wait()

        @pl.when(me > 0)
        def _():
            halo_copy(c).wait_recv()

        @pl.when((c > 0) & (me < n - 1))
        def _():
            halo_copy(c).wait_send()

        @pl.when(c + 2 < CHUNKS)
        def _():
            send_halo(c + 2)

    def store(c):
        return pltpu.make_async_copy(result.at[:, lanes_of(c)], out.at[:, lanes_of(c)], out_sem.at[c])

    def ready_third(c):
        load(c, 2).wait()
        looped(1, TEAM, lambda k: p_copy(c, k).wait_recv())

    def send_ends(c):
        looped(1, TEAM, lambda k: b_copy(c, k).start())
        brecv[c, rank] = bbuf[c, rank]

    def combine(c):
        looped(1, TEAM, lambda k: b_copy(c, k).wait_recv())
        a_re, a_im = owner_decay(c)
        state = jnp.zeros((16, quarter), f32), jnp.zeros((16, quarter), f32)
        for i in range(TEAM):
            state = advance(state, a_re, a_im, metas[i, 8:9, 0:1], brecv[c, i])
        lbuf[c, :16] = state[0].astype(bf16)
        lbuf[c, 16:] = state[1].astype(bf16)
        looped(1, teams, lambda k: later(k, lambda: l_copy(c, k).start()))

    def spread(c):
        looped(1, teams, lambda k: earlier(k, lambda: l_copy(c, k).wait_recv()))
        a_re, a_im = owner_decay(c)
        t_re, t_im = squared(a_re, a_im, TEAM.bit_length() - 1)

        def step(i, state):
            return advance(state, t_re, t_im, tflags[i][0:1, 0:1], lrecv[c, i])

        zero = jnp.zeros((16, quarter), f32)
        state = lax.fori_loop(0, team, step, (zero, zero))
        for i in range(TEAM):
            pbuf[c, i, :16] = state[0].astype(bf16)
            pbuf[c, i, 16:] = state[1].astype(bf16)
            if i < TEAM - 1:
                state = advance(state, a_re, a_im, metas[i, 8:9, 0:1], brecv[c, i])
        looped(1, TEAM, lambda k: p_copy(c, k).start())
        land[c, rank] = pbuf[c, rank]

    def step(s):
        def at(lag, fn, until=CHUNKS):
            @pl.when((s >= lag) & (s < until + lag))
            def _():
                fn(s - lag)

        def filters(c):
            ready_first(c)
            work(c, jnp.maximum(c - NEAR_LAG, 0), None)
            send_ends(c)

        def near_only(c):
            work(None, c, None)

        def far(c):
            ready_third(c)
            work(None, None, c)
            store(c).start()

        at(0, filters)

        @pl.when(s == 1)
        def _():
            team_flags()

        @pl.when(s == 2 * OWN_LAG)
        def _():
            looped(1, teams, lambda k: earlier(k, lambda: tflag_copy(k).wait_recv()))


        @pl.when((s >= CHUNKS) & (s < CHUNKS + NEAR_LAG))
        def _():
            near_only(s - NEAR_LAG)

        at(OWN_LAG, combine)
        at(2 * OWN_LAG, spread)
        at(3 * OWN_LAG, far)

    looped(0, CHUNKS + 3 * OWN_LAG, step)
    looped(0, CHUNKS, lambda c: store(c).wait())

    @pl.when(me < n - 1)
    def _():
        next_meta().wait_send()

    looped(1, teams, lambda k: later(k, lambda: tflag_copy(k).wait_send()))

    def drain(c):
        looped(1, TEAM, lambda k: b_copy(c, k).wait_send())
        looped(1, TEAM, lambda k: p_copy(c, k).wait_send())
        looped(1, teams, lambda k: later(k, lambda: l_copy(c, k).wait_send()))

    looped(0, CHUNKS, drain)


def shards(activations, gate_values, accepted, seg_starts, mr_taps, lr_rate, lr_angle, lr_residue):
    rows, width = activations.shape
    count, taps = mr_taps.shape
    modes = lr_rate.shape[1]
    n = lax.axis_size("seq")
    teams = n // TEAM
    span = width // CHUNKS
    quarter = span // TEAM
    tiles = span // LANES
    both = 2 * modes

    def dma(*shape):
        return pltpu.SemaphoreType.DMA(shape)

    hbm = pl.BlockSpec(memory_space=pltpu.HBM)
    mask = pltpu.VMEM((rows, LANES), bf16)
    return pl.pallas_call(
        functools.partial(kernel, n),
        in_specs=[hbm] * 8,
        out_specs=hbm,
        out_shape=jax.ShapeDtypeStruct((rows, width), bf16),
        scratch_shapes=[
            pltpu.VMEM((1, rows), jnp.int32), pltpu.VMEM((1, rows), jnp.int32), pltpu.VMEM((count, taps), bf16),
            pltpu.VMEM((modes, count), f32), pltpu.VMEM((modes, count), f32), pltpu.VMEM((2, modes, count), f32),
            pltpu.VMEM((rows, width), bf16), pltpu.VMEM((2, rows, width), bf16),
            pltpu.VMEM((rows, width), bf16), pltpu.VMEM((rows, width), bf16),
            pltpu.VMEM((count, taps), f32), pltpu.VMEM((rows, width), f32),
            pltpu.VMEM((count, taps), f32), pltpu.VMEM((width // LANES * 8, LANES), f32),
            pltpu.VMEM((4, modes, count), f32), pltpu.VMEM((both, count), f32),
            pltpu.VMEM((tiles, 8 * rows, 2 * rows), bf16), pltpu.VMEM((tiles, 4 * rows, 2 * rows), bf16),
            mask, mask, mask, mask, mask,
            pltpu.VMEM((16, LANES), f32), pltpu.VMEM((TEAM, 16, LANES), f32), pltpu.VMEM((16, LANES), f32),
            pltpu.VMEM((8, LANES), f32), pltpu.VMEM((teams, 8, LANES), f32),
            pltpu.VMEM((CHUNKS, TEAM, both, quarter), bf16), pltpu.VMEM((CHUNKS, TEAM, both, quarter), bf16),
            pltpu.VMEM((CHUNKS, both, quarter), bf16), pltpu.VMEM((CHUNKS, teams, both, quarter), bf16),
            pltpu.VMEM((CHUNKS, TEAM, both, quarter), bf16), pltpu.VMEM((CHUNKS, TEAM, both, quarter), bf16),
            pltpu.VMEM((rows, width), bf16),
            dma(6), dma(3, CHUNKS), dma(CHUNKS), dma(CHUNKS), dma(CHUNKS), dma(TEAM), dma(TEAM), dma(1), dma(1), dma(teams), dma(teams),
            dma(CHUNKS, TEAM), dma(CHUNKS, TEAM), dma(CHUNKS, teams), dma(CHUNKS, teams),
            dma(CHUNKS, TEAM), dma(CHUNKS, TEAM)],
        compiler_params=pltpu.CompilerParams(collective_id=0, has_side_effects=True,
                                             vmem_limit_bytes=54 * 2**20),
        name="hyena",
    )(activations, gate_values, accepted[None, :], seg_starts[None, :], mr_taps, lr_rate.T, lr_angle.T,
      jnp.swapaxes(lr_residue, 1, 2))


def solution(mesh):
    return jax.shard_map(
        shards,
        mesh=mesh,
        in_specs=(P(("groups", "seq"), None), P(None, ("groups", "seq"), None), P(("groups", "seq")),
                  P(("groups", "seq")), P(), P(), P(), P()),
        out_specs=P(("groups", "seq"), None),
        check_vma=False,
    )
```

```python
import functools
import jax
import jax.numpy as jnp
from jax import lax
from jax.experimental import pallas as pl
from jax.experimental.pallas import tpu as pltpu
from jax.sharding import PartitionSpec as P

f32 = jnp.float32
bf16 = jnp.bfloat16
MESH = pl.DeviceIdType.MESH
LANES = 128
TEAM = 4
CHUNKS = 8
PIECES = 4
NEAR_LAG = 2
LAGS = (1, 3, 5, 7, 8)


def iota(shape, dim):
    return lax.broadcasted_iota(jnp.int32, shape, dim)


def powers(re, im, exps, bits):
    on = (exps & 1) == 1
    out_re, out_im = jnp.where(on, re, 1.0), jnp.where(on, im, 0.0)
    for bit in range(1, bits):
        re, im = re * re - im * im, 2.0 * re * im
        on = ((exps >> bit) & 1) == 1
        new_re = out_re * re - out_im * im
        new_im = out_re * im + out_im * re
        out_re = jnp.where(on, new_re, out_re)
        out_im = jnp.where(on, new_im, out_im)
    return out_re, out_im


def squared(re, im, times):
    for _ in range(times):
        re, im = re * re - im * im, 2.0 * re * im
    return re, im


def outer(a_re, a_im, b_re, b_im, flip):
    res, ims = [], []
    for a in range(8):
        row = 7 - a if flip else a
        pr, pi = a_re[row : row + 1], a_im[row : row + 1]
        res.append(pr * b_re - pi * b_im)
        ims.append(pr * b_im + pi * b_re)
    return jnp.concatenate(res, 0), jnp.concatenate(ims, 0)


def circulant(row):
    wide = jnp.broadcast_to(row, (LANES, LANES))
    return pltpu.roll(wide, 1, 1, stride=1, stride_axis=0).astype(bf16)


def build_taps(taps, ma, mb, toep):
    for g in range(8):
        c = circulant(taps[g : g + 1, :])
        toep[g * 128 : (g + 1) * 128, :128] = c * ma[...]
        toep[g * 128 : (g + 1) * 128, 128:] = c * mb[...]


def build_tables(lam):
    lam_re, lam_im, res_re, res_im = lam[0:1], lam[1:2], lam[2:3], lam[3:4]
    a_re, a_im = powers(*squared(lam_re, lam_im, 4), iota((8, LANES), 0), 3)
    p_re, p_im = powers(lam_re, lam_im, 15 - iota((16, LANES), 0), 4)
    end_re, end_im = outer(a_re, a_im, p_re, p_im, True)
    real = res_re * end_re - res_im * end_im
    high = real.astype(bf16)
    low = (real - high.astype(f32)).astype(bf16)
    pick = (iota((8, LANES), 1) // 16 == iota((8, LANES), 0)).astype(bf16)
    near = lax.dot_general(jnp.concatenate([pick, pick], 1), jnp.concatenate([high, low], 1),
                           (((1,), (1,)), ((), ())), preferred_element_type=f32)
    return end_re.astype(bf16), end_im.astype(bf16), near.astype(bf16).astype(f32)


def mid_dot(prev, cur, gate, toep):
    full = jnp.dot(toep[...], jnp.concatenate([prev, cur], axis=0), preferred_element_type=f32)
    group = iota((128, LANES), 1) // 16
    mr = full[:128]
    for g in range(1, 8):
        mr = jnp.where(group == g, full[g * 128 : (g + 1) * 128], mr)
    return (gate.astype(f32) * mr).astype(bf16)


def ends_dot(mid, keep, end_re, end_im):
    kept = mid * keep[...]
    group16 = iota((16, LANES), 1) // 16
    parts = []
    for table in (end_re, end_im):
        whole = lax.dot_general(table, kept, (((0,), (0,)), ((), ())), preferred_element_type=f32)
        got = whole[:16]
        for g in range(1, 8):
            got = jnp.where(group16 == g, whole[g * 16 : (g + 1) * 16], got)
        parts.append(got)
    return jnp.concatenate(parts, 0).astype(bf16)


def build_near(near, mb, toep):
    for g in range(8):
        c = circulant(near[g : g + 1, :])
        half = (g % 2) * 128
        row = (g // 2) * 128
        toep[row : row + 128, half : half + 128] = c * mb[...]


def near_dot(mid, toep):
    group = iota((128, LANES), 1) // 16
    even = (group % 2 == 0).astype(bf16)
    window = jnp.concatenate([mid * even, mid * (1 - even)], axis=0)
    full = jnp.dot(toep[...], window, preferred_element_type=f32)
    lr = full[:128]
    for g in range(1, 4):
        lr = jnp.where(group // 2 == g, full[g * 128 : (g + 1) * 128], lr)
    return lr


def far_tile(lr, state, lam, gate, inside):
    lam_re, lam_im, res_re, res_im = lam[0:1], lam[1:2], lam[2:3], lam[3:4]
    a_re, a_im = powers(*squared(lam_re, lam_im, 4), iota((8, LANES), 0), 3)
    p_re, p_im = powers(lam_re, lam_im, iota((16, LANES), 0), 4)
    res_re, res_im = res_re * lam_re - res_im * lam_im, res_re * lam_im + res_im * lam_re
    q_re = res_re * p_re - res_im * p_im
    q_im = res_re * p_im + res_im * p_re
    in_re, in_im = outer(a_re, a_im, q_re, q_im, False)
    table = jnp.concatenate([in_re.astype(bf16) * inside[...], (-in_im).astype(bf16) * inside[...]], 1)
    group16 = iota((16, LANES), 1) // 16
    spread = []
    for ri in range(2):
        for g in range(8):
            spread.append(state[ri * 16 : (ri + 1) * 16, :] * (group16 == g).astype(bf16))
    lr = lr + jnp.dot(table, jnp.concatenate(spread, 0), preferred_element_type=f32)
    return (gate.astype(f32) * lr.astype(bf16).astype(f32)).astype(bf16)


def kernel(n, act_hbm, gates_hbm, acc_hbm, seg_hbm, taps_hbm, rate_hbm, angle_hbm, resid_hbm, out,
           acc, seg, taps, rate, angle, resid, act, gates, halo, mid, near, lr, back, lam, groups, lam_end, toep, toep_near,
           ma, mb_mr, mb_lr, keep, inside, meta, metas, prev_meta, tflag, tflags,
           bbuf, brecv, pair_own, pair_out, pair_in, pair_low, lbuf, lrecv, enter_own, enter_out, enter_in,
           pbuf, land,
           result, small_sem, in_sem, out_sem, hs, hr, ms, mr, ns, nr, ts, tr, bs, br, cs, cr, ls, lrs, es, er, ps, pr):
    rows, width = act.shape
    teams = n // TEAM
    span = width // CHUNKS
    quarter = span // TEAM
    tiles = span // LANES
    per_owner = tiles // TEAM
    me = lax.axis_index("seq")
    team = me // TEAM
    rank = lax.rem(me, TEAM)

    def looped(lo, hi, fn):
        def run(i, _):
            fn(i)
            return 0
        lax.fori_loop(lo, hi, run, 0)

    def mate(k):
        return team * TEAM + lax.rem(rank + k, TEAM)

    def peer(k):
        return lax.rem(me + k * TEAM, n)

    nxt, prv = lax.rem(me + 1, n), lax.rem(me + n - 1, n)
    barrier = pltpu.get_barrier_semaphore()

    def greet(to):
        pl.semaphore_signal(barrier, inc=1, device_id={"seq": to}, device_id_type=MESH)

    looped(1, TEAM, lambda k: greet(mate(k)))
    looped(1, teams, lambda k: greet(peer(k)))

    @pl.when(rank == TEAM - 1)
    def _():
        greet(nxt)

    @pl.when(rank == 0)
    def _():
        greet(prv)

    def lanes_of(c):
        return pl.ds(pl.multiple_of(c * span, LANES), span)

    def load(c, i):
        if i == 0:
            return pltpu.make_async_copy(act_hbm.at[:, lanes_of(c)], act.at[:, lanes_of(c)], in_sem.at[0, c])
        return pltpu.make_async_copy(gates_hbm.at[i - 1, :, lanes_of(c)], gates.at[i - 1, :, lanes_of(c)],
                                     in_sem.at[i, c])

    def fetch(i):
        src, dst = ((acc_hbm, acc), (seg_hbm, seg), (taps_hbm, taps), (rate_hbm, rate),
                    (angle_hbm, angle), (resid_hbm, resid))[i]
        return pltpu.make_async_copy(src, dst, small_sem.at[i])

    load(0, 0).start()
    for i in range(6):
        fetch(i).start()
    load(0, 1).start()
    looped(1, CHUNKS, lambda c: load(c, 0).start())
    looped(1, CHUNKS, lambda c: load(c, 1).start())
    looped(0, CHUNKS, lambda c: load(c, 2).start())

    def remote(src, dst, send, recv_sem, to):
        return pltpu.make_async_remote_copy(src_ref=src, dst_ref=dst, send_sem=send, recv_sem=recv_sem,
                                            device_id={"seq": to}, device_id_type=MESH)

    def halo_copy(c):
        return remote(act.at[:, lanes_of(c)], halo.at[:, lanes_of(c)], hs.at[c], hr.at[c], nxt)

    def next_meta():
        return remote(meta, prev_meta, ns.at[0], nr.at[0], nxt)

    def meta_copy(k):
        return remote(meta, metas.at[rank], ms.at[k], mr.at[k], mate(k))

    def tflag_copy(k):
        return remote(tflag, tflags.at[team], ts.at[k], tr.at[k], peer(k))

    chip, core = rank // 2, lax.rem(rank, 2)
    sibling = team * TEAM + chip * 2 + 1 - core
    across = team * TEAM + (1 - chip) * 2 + core

    def b_copy(c):
        return remote(bbuf.at[c, 1 - core], brecv.at[c, core], bs.at[c], br.at[c], sibling)

    def pair_copy(c):
        return remote(pair_out.at[c], pair_in.at[c], cs.at[c], cr.at[c], across)

    def l_copy(c, k):
        return remote(lbuf.at[c], lrecv.at[c, team], ls.at[c, k], lrs.at[c, k], peer(k))

    def enter_copy(c):
        return remote(enter_out.at[c], enter_in.at[c], es.at[c], er.at[c], across)

    def p_copy(c):
        return remote(pbuf.at[c], land.at[c, core], ps.at[c], pr.at[c], sibling)

    def send_halo(c):
        load(c, 0).wait()

        @pl.when(me < n - 1)
        def _():
            halo_copy(c).start()

    pl.semaphore_wait(barrier, TEAM - 1 + teams - 1 + (rank == 0).astype(jnp.int32)
                      + (rank == TEAM - 1).astype(jnp.int32))
    send_halo(0)

    fetch(0).wait()
    fetch(1).wait()
    first = jnp.transpose(jnp.broadcast_to((seg[...] - me * rows).astype(f32), (LANES, LANES)))
    last = first[LANES - 1 : LANES, :]
    own = acc[...].astype(f32)
    meta[:8] = jnp.broadcast_to(own, (8, LANES))
    meta[8:] = jnp.broadcast_to((last < 0).astype(f32), (8, LANES))

    @pl.when(me < n - 1)
    def _():
        next_meta().start()

    looped(1, TEAM, lambda k: meta_copy(k).start())
    t = iota((LANES, LANES), 0)
    j = iota((LANES, LANES), 1)
    tf, jf = t.astype(f32), j.astype(f32)
    within = ((j <= t) & (jf >= first)).astype(f32)
    mb_lr[...] = within.astype(bf16)
    mb_mr[...] = (within * own).astype(bf16)
    keep[...] = (tf >= last).astype(f32).astype(bf16)
    inside[...] = (first < 0).astype(f32).astype(bf16)
    prev_mask = ((j > t) & (jf - rows >= first)).astype(f32)

    for i in range(2, 6):
        fetch(i).wait()
    flip = (iota((LANES, LANES), 0) + iota((LANES, LANES), 1) == LANES - 1).astype(bf16)
    back[...] = jnp.dot(taps[...], flip, preferred_element_type=f32)
    mag = jnp.exp(-rate[...])
    scale = 0.25 * jnp.sqrt(rate[...])
    lam_re, lam_im = mag * jnp.cos(angle[...]), mag * jnp.sin(angle[...])
    groups[0] = lam_re
    groups[1] = lam_im
    groups[2] = scale * resid[0]
    groups[3] = scale * resid[1]
    end_re, end_im = squared(lam_re, lam_im, 7)
    lam_end[:16] = end_re
    lam_end[16:] = end_im
    group_lane = iota((16, LANES), 1) // 16
    diagonal = iota((16, LANES), 0) == lax.rem(iota((16, LANES), 1), 16)

    def pick_lanes(x, idx):
        return jnp.take_along_axis(x, idx, axis=1, mode="promise_in_bounds")

    blocks = groups.shape[2] // LANES

    def spread_lam(k):
        idx = group_lane + 8 * k
        picked = [[pick_lanes(groups[i, :, block * LANES : (block + 1) * LANES], idx) for i in range(4)]
                  for block in range(blocks)]
        for block in range(blocks):
            got = [jnp.sum(jnp.where(diagonal, x, 0.0), axis=0, keepdims=True) for x in picked[block]]
            got.append(jnp.zeros((4, LANES), f32))
            at = pl.ds(pl.multiple_of((block * 16 + k) * 8, 8), 8)
            lam[at, :] = jnp.concatenate(got, 0)

    looped(0, 16, spread_lam)

    @pl.when(me < n - 1)
    def _():
        halo_copy(0).wait_send()

    send_halo(1)

    @pl.when(me > 0)
    def _():
        next_meta().wait_recv()
        ma[...] = (prev_mask * prev_meta[0:1, :]).astype(bf16)

    @pl.when(me == 0)
    def _():
        ma[...] = jnp.zeros_like(ma)
        halo[...] = jnp.zeros_like(halo)

    def team_flags():
        looped(1, TEAM, lambda k: meta_copy(k).wait())
        metas[rank] = meta[...]
        whole = metas[0, 8:]
        for i in range(1, TEAM):
            whole = whole * metas[i, 8:]
        tflag[...] = whole
        looped(1, teams, lambda k: later(k, lambda: tflag_copy(k).start()))

    def later(k, fn):
        @pl.when(team + k < teams)
        def _():
            fn()

    def earlier(k, fn):
        @pl.when(team >= k)
        def _():
            fn()

    def owner_decay(c, quarter_of):
        res = []
        for i in range(per_owner):
            tile = c * tiles + quarter_of * per_owner + i
            block = tile // 16
            x = lam_end[:, pl.ds(pl.multiple_of(block * LANES, LANES), LANES)]
            idx = iota((32, LANES), 1) // 16 + 8 * lax.rem(tile, 16)
            res.append(pick_lanes(x, idx))
        d = jnp.concatenate(res, 1)
        return d[:16], d[16:]

    def advance(state, a_re, a_im, go, piece):
        s_re, s_im = state
        piece = piece.astype(f32)
        f_re, f_im = a_re * go, a_im * go
        return f_re * s_re - f_im * s_im + piece[:16], f_re * s_im + f_im * s_re + piece[16:]

    def where_of(c):
        where = []
        for k in range(tiles):
            tile = c * tiles + k
            where.append((pl.ds(pl.multiple_of(tile * LANES, LANES), LANES),
                          pl.ds(pl.multiple_of(tile * 8, 8), 8),
                          k // per_owner,
                          pl.ds(k % per_owner * LANES, LANES)))
        return where

    def work(c1, c2, c3):
        stores = []
        if c1 is not None:
            where1 = where_of(c1)
            tables = [build_tables(lam[eight, :]) for lanes, eight, owner, local in where1]
            mids = []
            for u in range(tiles + 1):
                if u < tiles:
                    build_taps(back[where1[u][1], :], ma, mb_mr, toep.at[u])
                if u >= 1:
                    lanes = where1[u - 1][0]
                    mids.append(mid_dot(halo[:, lanes], act[:, lanes], gates[0, :, lanes], toep.at[u - 1]))
            ends = [ends_dot(m, keep, tb[0], tb[1]) for m, tb in zip(mids, tables)]
        if c3 is not None:
            where3 = where_of(c3)
            outs = [far_tile(lr[:, lanes], land[c3, owner % 2, owner // 2, :, local], lam[eight, :],
                             gates[1, :, lanes], inside) for lanes, eight, owner, local in where3]
        if c2 is not None:
            where2 = where_of(c2)
            for u, (lanes, eight, owner, local) in enumerate(where2):
                build_near(near[eight, :], mb_lr, toep_near.at[u])
            lrs = [near_dot(mid[:, lanes], toep_near.at[u])
                   for u, (lanes, eight, owner, local) in enumerate(where2)]
        if c3 is not None:
            for (lanes, eight, owner, local), o in zip(where3, outs):
                result[:, lanes] = o
        if c2 is not None:
            for (lanes, eight, owner, local), o in zip(where2, lrs):
                lr[:, lanes] = o
        if c1 is not None:
            for (lanes, eight, owner, local), m, b, tb in zip(where1, mids, ends, tables):
                mid[:, lanes] = m
                bbuf[c1, owner % 2, owner // 2, :, local] = b
                near[eight, :] = tb[2]

    def ready_first(c):
        load(c, 1).wait()

        @pl.when(me > 0)
        def _():
            halo_copy(c).wait_recv()


    def store(c):
        return pltpu.make_async_copy(result.at[:, lanes_of(c)], out.at[:, lanes_of(c)], out_sem.at[c])

    def ready_third(c):
        load(c, 2).wait()
        p_copy(c).wait_recv()

    def send_ends(c):
        b_copy(c).start()
        brecv[c, core] = bbuf[c, core]

    def flag(i):
        return metas[i, 8:9, 0:1]

    def split(x):
        return x[:16].astype(f32), x[16:].astype(f32)

    def put(ref, c, state):
        ref[c, :16] = state[0].astype(ref.dtype)
        ref[c, 16:] = state[1].astype(ref.dtype)

    def pair(c):
        b_copy(c).wait_recv()
        for out_ref, half in ((pair_own, chip), (pair_out, 1 - chip)):
            a_re, a_im = owner_decay(c, 2 * half + core)
            put(out_ref, c, advance(split(brecv[c, 0, half]), a_re, a_im, flag(chip * 2 + 1), brecv[c, 1, half]))
        pair_copy(c).start()

    def combine(c):
        pair_copy(c).wait_recv()
        a_re, a_im = squared(*owner_decay(c, rank), 1)
        mine, other = pair_own[c], pair_in[c].astype(f32)
        low = jnp.where(chip == 0, mine, other)
        high = jnp.where(chip == 0, other, mine)
        pair_low[c] = low
        put(lbuf, c, advance(split(low), a_re, a_im, flag(2) * flag(3), high))
        looped(1, teams, lambda k: later(k, lambda: l_copy(c, k).start()))

    def spread(c):
        looped(1, teams, lambda k: earlier(k, lambda: l_copy(c, k).wait_recv()))
        a_re, a_im = squared(*owner_decay(c, rank), 1)
        t_re, t_im = squared(a_re, a_im, 1)

        def add(i, state):
            return advance(state, t_re, t_im, tflags[i][0:1, 0:1], lrecv[c, i])

        zero = jnp.zeros((16, quarter), f32)
        state = lax.fori_loop(0, team, add, (zero, zero))
        after = advance(state, a_re, a_im, flag(0) * flag(1), pair_low[c])
        here = [jnp.where(chip == 0, x, y) for x, y in zip(state, after)]
        there = [jnp.where(chip == 0, y, x) for x, y in zip(state, after)]
        put(enter_own, c, here)
        put(enter_out, c, there)
        enter_copy(c).start()

    def share(c):
        enter_copy(c).wait_recv()
        for src, half in ((enter_own, chip), (enter_in, 1 - chip)):
            state = split(src[c])
            a_re, a_im = owner_decay(c, 2 * half + core)
            after = advance(state, a_re, a_im, flag(chip * 2), brecv[c, 0, half])
            here = [jnp.where(core == 0, x, y) for x, y in zip(state, after)]
            there = [jnp.where(core == 0, y, x) for x, y in zip(state, after)]
            land[c, core, half, :16] = here[0].astype(bf16)
            land[c, core, half, 16:] = here[1].astype(bf16)
            pbuf[c, half, :16] = there[0].astype(bf16)
            pbuf[c, half, 16:] = there[1].astype(bf16)
        p_copy(c).start()

    def step(s):
        def at(lag, fn, until=CHUNKS):
            @pl.when((s >= lag) & (s < until + lag))
            def _():
                fn(s - lag)

        def filters(c):
            ready_first(c)
            work(c, jnp.maximum(c - NEAR_LAG, 0), None)
            send_ends(c)

        def near_only(c):
            work(None, c, None)

        def far(c):
            ready_third(c)
            work(None, None, c)
            store(c).start()

        def push(c):
            @pl.when((c > 0) & (me < n - 1))
            def _():
                halo_copy(c).wait_send()

            @pl.when(c + 2 < CHUNKS)
            def _():
                send_halo(c + 2)

        at(0, filters)

        @pl.when(s == 0)
        def _():
            team_flags()

        @pl.when(s == LAGS[2])
        def _():
            looped(1, teams, lambda k: earlier(k, lambda: tflag_copy(k).wait_recv()))


        @pl.when((s >= CHUNKS) & (s < CHUNKS + NEAR_LAG))
        def _():
            near_only(s - NEAR_LAG)

        at(LAGS[0], pair)
        at(LAGS[1], combine)
        at(LAGS[2], spread)
        at(LAGS[3], share)
        at(0, push)
        at(LAGS[4], far)

    looped(0, CHUNKS + LAGS[4], step)
    looped(0, CHUNKS, lambda c: store(c).wait())

    @pl.when(me < n - 1)
    def _():
        next_meta().wait_send()

    looped(1, teams, lambda k: later(k, lambda: tflag_copy(k).wait_send()))

    def drain(c):
        b_copy(c).wait_send()
        pair_copy(c).wait_send()
        enter_copy(c).wait_send()
        p_copy(c).wait_send()
        looped(1, teams, lambda k: later(k, lambda: l_copy(c, k).wait_send()))

    looped(0, CHUNKS, drain)


def hand_over(src, dst, held, in_sem, out_sem):
    size = src.shape[0] // PIECES
    at = [pl.ds(i * size, size) for i in range(PIECES)]
    loads = [pltpu.make_async_copy(src.at[a], held.at[a], in_sem.at[i]) for i, a in enumerate(at)]
    saves = [pltpu.make_async_copy(held.at[a], dst.at[a], out_sem.at[i]) for i, a in enumerate(at)]
    for c in loads:
        c.start()
    for c, d in zip(loads, saves):
        c.wait()
        d.start()
    for d in saves:
        d.wait()


def shards(activations, gate_values, accepted, seg_starts, mr_taps, lr_rate, lr_angle, lr_residue):
    rows, width = activations.shape
    count, taps = mr_taps.shape
    modes = lr_rate.shape[1]
    n = lax.axis_size("seq")
    teams = n // TEAM
    span = width // CHUNKS
    quarter = span // TEAM
    tiles = span // LANES
    both = 2 * modes

    def dma(*shape):
        return pltpu.SemaphoreType.DMA(shape)

    hbm = pl.BlockSpec(memory_space=pltpu.HBM)
    mask = pltpu.VMEM((rows, LANES), bf16)
    part, part32 = pltpu.VMEM((CHUNKS, both, quarter), bf16), pltpu.VMEM((CHUNKS, both, quarter), f32)
    four = pltpu.VMEM((CHUNKS, 2, 2, both, quarter), bf16)
    gated = pl.pallas_call(
        functools.partial(kernel, n),
        in_specs=[hbm] * 8,
        out_specs=hbm,
        out_shape=jax.ShapeDtypeStruct((rows, width), bf16),
        scratch_shapes=[
            pltpu.VMEM((1, rows), jnp.int32), pltpu.VMEM((1, rows), jnp.int32), pltpu.VMEM((count, taps), bf16),
            pltpu.VMEM((modes, count), f32), pltpu.VMEM((modes, count), f32), pltpu.VMEM((2, modes, count), f32),
            pltpu.VMEM((rows, width), bf16), pltpu.VMEM((2, rows, width), bf16),
            pltpu.VMEM((rows, width), bf16), pltpu.VMEM((rows, width), bf16),
            pltpu.VMEM((count, taps), f32), pltpu.VMEM((rows, width), f32),
            pltpu.VMEM((count, taps), f32), pltpu.VMEM((width // LANES * 8, LANES), f32),
            pltpu.VMEM((4, modes, count), f32), pltpu.VMEM((both, count), f32),
            pltpu.VMEM((tiles, 8 * rows, 2 * rows), bf16), pltpu.VMEM((tiles, 4 * rows, 2 * rows), bf16),
            mask, mask, mask, mask, mask,
            pltpu.VMEM((16, LANES), f32), pltpu.VMEM((TEAM, 16, LANES), f32), pltpu.VMEM((16, LANES), f32),
            pltpu.VMEM((8, LANES), f32), pltpu.VMEM((teams, 8, LANES), f32),
            four, four, part32, part, part, part32,
            part, pltpu.VMEM((CHUNKS, teams, both, quarter), bf16), part32, part, part,
            pltpu.VMEM((CHUNKS, 2, both, quarter), bf16), four,
            pltpu.VMEM((rows, width), bf16),
            dma(6), dma(3, CHUNKS), dma(CHUNKS), dma(CHUNKS), dma(CHUNKS), dma(TEAM), dma(TEAM), dma(1), dma(1), dma(teams), dma(teams),
            dma(CHUNKS), dma(CHUNKS), dma(CHUNKS), dma(CHUNKS), dma(CHUNKS, teams), dma(CHUNKS, teams),
            dma(CHUNKS), dma(CHUNKS), dma(CHUNKS), dma(CHUNKS)],
        compiler_params=pltpu.CompilerParams(collective_id=0, has_side_effects=True,
                                             vmem_limit_bytes=54 * 2**20),
        name="hyena",
    )(activations, gate_values, accepted[None, :], seg_starts[None, :], mr_taps, lr_rate.T, lr_angle.T,
      jnp.swapaxes(lr_residue, 1, 2))
    return pl.pallas_call(
        hand_over,
        in_specs=[hbm],
        out_specs=hbm,
        out_shape=jax.ShapeDtypeStruct((rows, width), bf16),
        scratch_shapes=[pltpu.VMEM((rows, width), bf16), dma(PIECES), dma(PIECES)],
        compiler_params=pltpu.CompilerParams(vmem_limit_bytes=58 * 2**20),
        name="hand_over",
    )(gated)


def solution(mesh):
    return jax.shard_map(
        shards,
        mesh=mesh,
        in_specs=(P(("groups", "seq"), None), P(None, ("groups", "seq"), None), P(("groups", "seq")),
                  P(("groups", "seq")), P(), P(), P(), P()),
        out_specs=P(("groups", "seq"), None),
        check_vma=False,
    )
```

```python
import functools
import jax
import jax.numpy as jnp
from jax import lax
from jax.experimental import pallas as pl
from jax.experimental.pallas import tpu as pltpu
from jax.sharding import PartitionSpec as P

f32 = jnp.float32
bf16 = jnp.bfloat16
MESH = pl.DeviceIdType.MESH
LANES = 128
TEAM = 4
CHUNKS = 8
PIECES = 4
NEAR_LAG = 2
LAGS = (1, 3, 5, 7, 8)


def iota(shape, dim):
    return lax.broadcasted_iota(jnp.int32, shape, dim)


def powers(re, im, exps, bits):
    on = (exps & 1) == 1
    out_re, out_im = jnp.where(on, re, 1.0), jnp.where(on, im, 0.0)
    for bit in range(1, bits):
        re, im = re * re - im * im, 2.0 * re * im
        on = ((exps >> bit) & 1) == 1
        new_re = out_re * re - out_im * im
        new_im = out_re * im + out_im * re
        out_re = jnp.where(on, new_re, out_re)
        out_im = jnp.where(on, new_im, out_im)
    return out_re, out_im


def squared(re, im, times):
    for _ in range(times):
        re, im = re * re - im * im, 2.0 * re * im
    return re, im


def outer(a_re, a_im, b_re, b_im, flip):
    res, ims = [], []
    for a in range(8):
        row = 7 - a if flip else a
        pr, pi = a_re[row : row + 1], a_im[row : row + 1]
        res.append(pr * b_re - pi * b_im)
        ims.append(pr * b_im + pi * b_re)
    return jnp.concatenate(res, 0), jnp.concatenate(ims, 0)


def circulant(row):
    wide = jnp.broadcast_to(row, (LANES, LANES))
    return pltpu.roll(wide, 1, 1, stride=1, stride_axis=0).astype(bf16)


def build_taps(taps, ma, mb, toep):
    for g in range(8):
        c = circulant(taps[g : g + 1, :])
        toep[g * 128 : (g + 1) * 128, :128] = c * ma[...]
        toep[g * 128 : (g + 1) * 128, 128:] = c * mb[...]


def build_tables(lam):
    lam_re, lam_im, res_re, res_im = lam[0:1], lam[1:2], lam[2:3], lam[3:4]
    a_re, a_im = powers(*squared(lam_re, lam_im, 4), iota((8, LANES), 0), 3)
    p_re, p_im = powers(lam_re, lam_im, 15 - iota((16, LANES), 0), 4)
    end_re, end_im = outer(a_re, a_im, p_re, p_im, True)
    real = res_re * end_re - res_im * end_im
    high = real.astype(bf16)
    low = (real - high.astype(f32)).astype(bf16)
    pick = (iota((8, LANES), 1) // 16 == iota((8, LANES), 0)).astype(bf16)
    near = lax.dot_general(jnp.concatenate([pick, pick], 1), jnp.concatenate([high, low], 1),
                           (((1,), (1,)), ((), ())), preferred_element_type=f32)
    return end_re.astype(bf16), end_im.astype(bf16), near.astype(bf16).astype(f32)


def mid_dot(prev, cur, gate, toep):
    full = jnp.dot(toep[...], jnp.concatenate([prev, cur], axis=0), preferred_element_type=f32)
    group = iota((128, LANES), 1) // 16
    mr = full[:128]
    for g in range(1, 8):
        mr = jnp.where(group == g, full[g * 128 : (g + 1) * 128], mr)
    return (gate.astype(f32) * mr).astype(bf16)


def ends_dot(mid, keep, end_re, end_im):
    kept = mid * keep[...]
    group16 = iota((16, LANES), 1) // 16
    parts = []
    for table in (end_re, end_im):
        whole = lax.dot_general(table, kept, (((0,), (0,)), ((), ())), preferred_element_type=f32)
        got = whole[:16]
        for g in range(1, 8):
            got = jnp.where(group16 == g, whole[g * 16 : (g + 1) * 16], got)
        parts.append(got)
    return jnp.concatenate(parts, 0).astype(bf16)


def build_near(near, mb, toep):
    for g in range(8):
        c = circulant(near[g : g + 1, :])
        half = (g % 2) * 128
        row = (g // 2) * 128
        toep[row : row + 128, half : half + 128] = c * mb[...]


def near_dot(mid, toep):
    group = iota((128, LANES), 1) // 16
    even = (group % 2 == 0).astype(bf16)
    window = jnp.concatenate([mid * even, mid * (1 - even)], axis=0)
    full = jnp.dot(toep[...], window, preferred_element_type=f32)
    lr = full[:128]
    for g in range(1, 4):
        lr = jnp.where(group // 2 == g, full[g * 128 : (g + 1) * 128], lr)
    return lr


def far_tile(lr, state, lam, gate, inside):
    lam_re, lam_im, res_re, res_im = lam[0:1], lam[1:2], lam[2:3], lam[3:4]
    a_re, a_im = powers(*squared(lam_re, lam_im, 4), iota((8, LANES), 0), 3)
    p_re, p_im = powers(lam_re, lam_im, iota((16, LANES), 0), 4)
    res_re, res_im = res_re * lam_re - res_im * lam_im, res_re * lam_im + res_im * lam_re
    q_re = res_re * p_re - res_im * p_im
    q_im = res_re * p_im + res_im * p_re
    in_re, in_im = outer(a_re, a_im, q_re, q_im, False)
    table = jnp.concatenate([in_re.astype(bf16) * inside[...], (-in_im).astype(bf16) * inside[...]], 1)
    group16 = iota((16, LANES), 1) // 16
    spread = []
    for ri in range(2):
        for g in range(8):
            spread.append(state[ri * 16 : (ri + 1) * 16, :] * (group16 == g).astype(bf16))
    lr = lr + jnp.dot(table, jnp.concatenate(spread, 0), preferred_element_type=f32)
    return (gate.astype(f32) * lr.astype(bf16).astype(f32)).astype(bf16)


def kernel(n, act_hbm, gates_hbm, acc_hbm, seg_hbm, taps_hbm, rate_hbm, angle_hbm, resid_hbm, out,
           acc, seg, taps, rate, angle, resid, act, gates, halo, mid, near, lr, back, lam, groups, lam_end, toep, toep_near,
           ma, mb_mr, mb_lr, keep, inside, meta, metas, prev_meta, tflag, tflags,
           bbuf, brecv, pair_own, pair_out, pair_in, pair_low, lbuf, lrecv, enter_own, enter_out, enter_in,
           pbuf, land,
           result, small_sem, in_sem, out_sem, hs, hr, ms, mr, ns, nr, ts, tr, bs, br, cs, cr, ls, lrs, es, er, ps, pr):
    rows, width = act.shape
    teams = n // TEAM
    span = width // CHUNKS
    quarter = span // TEAM
    tiles = span // LANES
    per_owner = tiles // TEAM
    me = lax.axis_index("seq")
    team = me // TEAM
    rank = lax.rem(me, TEAM)

    def looped(lo, hi, fn):
        def run(i, _):
            fn(i)
            return 0
        lax.fori_loop(lo, hi, run, 0)

    def mate(k):
        return team * TEAM + lax.rem(rank + k, TEAM)

    def peer(k):
        return lax.rem(me + k * TEAM, n)

    nxt, prv = lax.rem(me + 1, n), lax.rem(me + n - 1, n)
    barrier = pltpu.get_barrier_semaphore()

    def greet(to):
        pl.semaphore_signal(barrier, inc=1, device_id={"seq": to}, device_id_type=MESH)

    looped(1, TEAM, lambda k: greet(mate(k)))
    looped(1, teams, lambda k: greet(peer(k)))

    @pl.when(rank == TEAM - 1)
    def _():
        greet(nxt)

    @pl.when(rank == 0)
    def _():
        greet(prv)

    def lanes_of(c):
        return pl.ds(pl.multiple_of(c * span, LANES), span)

    def load(c, i):
        if i == 0:
            return pltpu.make_async_copy(act_hbm.at[:, lanes_of(c)], act.at[:, lanes_of(c)], in_sem.at[0, c])
        return pltpu.make_async_copy(gates_hbm.at[i - 1, :, lanes_of(c)], gates.at[i - 1, :, lanes_of(c)],
                                     in_sem.at[i, c])

    def fetch(i):
        src, dst = ((acc_hbm, acc), (seg_hbm, seg), (taps_hbm, taps), (rate_hbm, rate),
                    (angle_hbm, angle), (resid_hbm, resid))[i]
        return pltpu.make_async_copy(src, dst, small_sem.at[i])

    load(0, 0).start()
    for i in range(6):
        fetch(i).start()
    load(0, 1).start()
    looped(1, CHUNKS, lambda c: load(c, 0).start())
    looped(1, CHUNKS, lambda c: load(c, 1).start())
    looped(0, CHUNKS, lambda c: load(c, 2).start())

    def remote(src, dst, send, recv_sem, to):
        return pltpu.make_async_remote_copy(src_ref=src, dst_ref=dst, send_sem=send, recv_sem=recv_sem,
                                            device_id={"seq": to}, device_id_type=MESH)

    def halo_copy(c):
        return remote(act.at[:, lanes_of(c)], halo.at[:, lanes_of(c)], hs.at[c], hr.at[c], nxt)

    def next_meta():
        return remote(meta, prev_meta, ns.at[0], nr.at[0], nxt)

    def meta_copy(k):
        return remote(meta, metas.at[rank], ms.at[k], mr.at[k], mate(k))

    def tflag_copy(k):
        return remote(tflag, tflags.at[team], ts.at[k], tr.at[k], peer(k))

    chip, core = rank // 2, lax.rem(rank, 2)
    sibling = team * TEAM + chip * 2 + 1 - core
    across = team * TEAM + (1 - chip) * 2 + core

    def b_copy(c):
        return remote(bbuf.at[c, 1 - core], brecv.at[c, core], bs.at[c], br.at[c], sibling)

    def pair_copy(c):
        return remote(pair_out.at[c], pair_in.at[c], cs.at[c], cr.at[c], across)

    def l_copy(c, k):
        return remote(lbuf.at[c], lrecv.at[c, team], ls.at[c, k], lrs.at[c, k], peer(k))

    def enter_copy(c):
        return remote(enter_out.at[c], enter_in.at[c], es.at[c], er.at[c], across)

    def p_copy(c):
        return remote(pbuf.at[c], land.at[c, core], ps.at[c], pr.at[c], sibling)

    def send_halo(c):
        load(c, 0).wait()

        @pl.when(me < n - 1)
        def _():
            halo_copy(c).start()

    pl.semaphore_wait(barrier, TEAM - 1 + teams - 1 + (rank == 0).astype(jnp.int32)
                      + (rank == TEAM - 1).astype(jnp.int32))
    send_halo(0)

    fetch(0).wait()
    fetch(1).wait()
    first = jnp.transpose(jnp.broadcast_to((seg[...] - me * rows).astype(f32), (LANES, LANES)))
    last = first[LANES - 1 : LANES, :]
    own = acc[...].astype(f32)
    meta[:8] = jnp.broadcast_to(own, (8, LANES))
    meta[8:] = jnp.broadcast_to((last < 0).astype(f32), (8, LANES))

    @pl.when(me < n - 1)
    def _():
        next_meta().start()

    looped(1, TEAM, lambda k: meta_copy(k).start())
    t = iota((LANES, LANES), 0)
    j = iota((LANES, LANES), 1)
    tf, jf = t.astype(f32), j.astype(f32)
    within = ((j <= t) & (jf >= first)).astype(f32)
    mb_lr[...] = within.astype(bf16)
    mb_mr[...] = (within * own).astype(bf16)
    keep[...] = (tf >= last).astype(f32).astype(bf16)
    inside[...] = (first < 0).astype(f32).astype(bf16)
    prev_mask = ((j > t) & (jf - rows >= first)).astype(f32)

    for i in range(2, 6):
        fetch(i).wait()
    flip = (iota((LANES, LANES), 0) + iota((LANES, LANES), 1) == LANES - 1).astype(bf16)
    back[...] = jnp.dot(taps[...], flip, preferred_element_type=f32)
    mag = jnp.exp(-rate[...])
    scale = 0.25 * jnp.sqrt(rate[...])
    lam_re, lam_im = mag * jnp.cos(angle[...]), mag * jnp.sin(angle[...])
    groups[0] = lam_re
    groups[1] = lam_im
    groups[2] = scale * resid[0]
    groups[3] = scale * resid[1]
    end_re, end_im = squared(lam_re, lam_im, 7)
    lam_end[:16] = end_re
    lam_end[16:] = end_im
    group_lane = iota((16, LANES), 1) // 16
    diagonal = iota((16, LANES), 0) == lax.rem(iota((16, LANES), 1), 16)

    def pick_lanes(x, idx):
        return jnp.take_along_axis(x, idx, axis=1, mode="promise_in_bounds")

    blocks = groups.shape[2] // LANES

    def spread_lam(k):
        idx = group_lane + 8 * k
        picked = [[pick_lanes(groups[i, :, block * LANES : (block + 1) * LANES], idx) for i in range(4)]
                  for block in range(blocks)]
        for block in range(blocks):
            got = [jnp.sum(jnp.where(diagonal, x, 0.0), axis=0, keepdims=True) for x in picked[block]]
            got.append(jnp.zeros((4, LANES), f32))
            at = pl.ds(pl.multiple_of((block * 16 + k) * 8, 8), 8)
            lam[at, :] = jnp.concatenate(got, 0)

    looped(0, 16, spread_lam)

    @pl.when(me < n - 1)
    def _():
        halo_copy(0).wait_send()

    send_halo(1)

    @pl.when(me > 0)
    def _():
        next_meta().wait_recv()
        ma[...] = (prev_mask * prev_meta[0:1, :]).astype(bf16)

    @pl.when(me == 0)
    def _():
        ma[...] = jnp.zeros_like(ma)
        halo[...] = jnp.zeros_like(halo)

    def team_flags():
        looped(1, TEAM, lambda k: meta_copy(k).wait())
        metas[rank] = meta[...]
        whole = metas[0, 8:]
        for i in range(1, TEAM):
            whole = whole * metas[i, 8:]
        tflag[...] = whole
        looped(1, teams, lambda k: later(k, lambda: tflag_copy(k).start()))

    def later(k, fn):
        @pl.when(team + k < teams)
        def _():
            fn()

    def earlier(k, fn):
        @pl.when(team >= k)
        def _():
            fn()

    def owner_decay(c, quarter_of):
        res = []
        for i in range(per_owner):
            tile = c * tiles + quarter_of * per_owner + i
            block = tile // 16
            x = lam_end[:, pl.ds(pl.multiple_of(block * LANES, LANES), LANES)]
            idx = iota((32, LANES), 1) // 16 + 8 * lax.rem(tile, 16)
            res.append(pick_lanes(x, idx))
        d = jnp.concatenate(res, 1)
        return d[:16], d[16:]

    def advance(state, a_re, a_im, go, piece):
        s_re, s_im = state
        piece = piece.astype(f32)
        f_re, f_im = a_re * go, a_im * go
        return f_re * s_re - f_im * s_im + piece[:16], f_re * s_im + f_im * s_re + piece[16:]

    def where_of(c):
        where = []
        for k in range(tiles):
            tile = c * tiles + k
            where.append((pl.ds(pl.multiple_of(tile * LANES, LANES), LANES),
                          pl.ds(pl.multiple_of(tile * 8, 8), 8),
                          k // per_owner,
                          pl.ds(k % per_owner * LANES, LANES)))
        return where

    def work(c1, c2, c3):
        stores = []
        if c1 is not None:
            where1 = where_of(c1)
            tables = [build_tables(lam[eight, :]) for lanes, eight, owner, local in where1]
            mids = []
            for u in range(tiles + 1):
                if u < tiles:
                    build_taps(back[where1[u][1], :], ma, mb_mr, toep.at[u])
                if u >= 1:
                    lanes = where1[u - 1][0]
                    mids.append(mid_dot(halo[:, lanes], act[:, lanes], gates[0, :, lanes], toep.at[u - 1]))
            ends = [ends_dot(m, keep, tb[0], tb[1]) for m, tb in zip(mids, tables)]
        if c3 is not None:
            where3 = where_of(c3)
            outs = [far_tile(lr[:, lanes], land[c3, owner % 2, owner // 2, :, local], lam[eight, :],
                             gates[1, :, lanes], inside) for lanes, eight, owner, local in where3]
        if c2 is not None:
            where2 = where_of(c2)
            for u, (lanes, eight, owner, local) in enumerate(where2):
                build_near(near[eight, :], mb_lr, toep_near.at[u])
            lrs = [near_dot(mid[:, lanes], toep_near.at[u])
                   for u, (lanes, eight, owner, local) in enumerate(where2)]
        if c3 is not None:
            for (lanes, eight, owner, local), o in zip(where3, outs):
                result[:, lanes] = o
        if c2 is not None:
            for (lanes, eight, owner, local), o in zip(where2, lrs):
                lr[:, lanes] = o
        if c1 is not None:
            for (lanes, eight, owner, local), m, b, tb in zip(where1, mids, ends, tables):
                mid[:, lanes] = m
                bbuf[c1, owner % 2, owner // 2, :, local] = b
                near[eight, :] = tb[2]

    def ready_first(c):
        load(c, 1).wait()

        @pl.when(me > 0)
        def _():
            halo_copy(c).wait_recv()


    def store(c):
        return pltpu.make_async_copy(result.at[:, lanes_of(c)], out.at[:, lanes_of(c)], out_sem.at[c])

    def ready_third(c):
        load(c, 2).wait()
        p_copy(c).wait_recv()

    def send_ends(c):
        b_copy(c).start()
        brecv[c, core] = bbuf[c, core]

    def flag(i):
        return metas[i, 8:9, 0:1]

    def split(x):
        return x[:16].astype(f32), x[16:].astype(f32)

    def put(ref, c, state):
        ref[c, :16] = state[0].astype(ref.dtype)
        ref[c, 16:] = state[1].astype(ref.dtype)

    def pair(c):
        b_copy(c).wait_recv()
        for out_ref, half in ((pair_own, chip), (pair_out, 1 - chip)):
            a_re, a_im = owner_decay(c, 2 * half + core)
            put(out_ref, c, advance(split(brecv[c, 0, half]), a_re, a_im, flag(chip * 2 + 1), brecv[c, 1, half]))
        pair_copy(c).start()

    def combine(c):
        pair_copy(c).wait_recv()
        a_re, a_im = squared(*owner_decay(c, rank), 1)
        mine, other = pair_own[c], pair_in[c].astype(f32)
        low = jnp.where(chip == 0, mine, other)
        high = jnp.where(chip == 0, other, mine)
        pair_low[c] = low
        put(lbuf, c, advance(split(low), a_re, a_im, flag(2) * flag(3), high))
        looped(1, teams, lambda k: later(k, lambda: l_copy(c, k).start()))

    def spread(c):
        looped(1, teams, lambda k: earlier(k, lambda: l_copy(c, k).wait_recv()))
        a_re, a_im = squared(*owner_decay(c, rank), 1)
        t_re, t_im = squared(a_re, a_im, 1)

        def add(i, state):
            return advance(state, t_re, t_im, tflags[i][0:1, 0:1], lrecv[c, i])

        zero = jnp.zeros((16, quarter), f32)
        state = lax.fori_loop(0, team, add, (zero, zero))
        after = advance(state, a_re, a_im, flag(0) * flag(1), pair_low[c])
        here = [jnp.where(chip == 0, x, y) for x, y in zip(state, after)]
        there = [jnp.where(chip == 0, y, x) for x, y in zip(state, after)]
        put(enter_own, c, here)
        put(enter_out, c, there)
        enter_copy(c).start()

    def share(c):
        enter_copy(c).wait_recv()
        for src, half in ((enter_own, chip), (enter_in, 1 - chip)):
            state = split(src[c])
            a_re, a_im = owner_decay(c, 2 * half + core)
            after = advance(state, a_re, a_im, flag(chip * 2), brecv[c, 0, half])
            here = [jnp.where(core == 0, x, y) for x, y in zip(state, after)]
            there = [jnp.where(core == 0, y, x) for x, y in zip(state, after)]
            land[c, core, half, :16] = here[0].astype(bf16)
            land[c, core, half, 16:] = here[1].astype(bf16)
            pbuf[c, half, :16] = there[0].astype(bf16)
            pbuf[c, half, 16:] = there[1].astype(bf16)
        p_copy(c).start()

    def step(s):
        def at(lag, fn, until=CHUNKS):
            @pl.when((s >= lag) & (s < until + lag))
            def _():
                fn(s - lag)

        def filters(c):
            ready_first(c)
            work(c, None, None)
            send_ends(c)

        def near_only(c):
            work(None, c, None)

        def far(c):
            ready_third(c)
            work(None, None, c)
            store(c).start()

        def push(c):
            @pl.when((c > 0) & (me < n - 1))
            def _():
                halo_copy(c).wait_send()

            @pl.when(c + 2 < CHUNKS)
            def _():
                send_halo(c + 2)

        at(0, filters)

        @pl.when(s == 0)
        def _():
            team_flags()

        @pl.when(s == LAGS[2])
        def _():
            looped(1, teams, lambda k: earlier(k, lambda: tflag_copy(k).wait_recv()))


        at(NEAR_LAG, near_only)
        at(LAGS[0], pair)
        at(LAGS[1], combine)
        at(LAGS[2], spread)
        at(LAGS[3], share)
        at(0, push)
        at(LAGS[4], far)

    looped(0, CHUNKS + LAGS[4], step)
    looped(0, CHUNKS, lambda c: store(c).wait())

    @pl.when(me < n - 1)
    def _():
        next_meta().wait_send()

    looped(1, teams, lambda k: later(k, lambda: tflag_copy(k).wait_send()))

    def drain(c):
        b_copy(c).wait_send()
        pair_copy(c).wait_send()
        enter_copy(c).wait_send()
        p_copy(c).wait_send()
        looped(1, teams, lambda k: later(k, lambda: l_copy(c, k).wait_send()))

    looped(0, CHUNKS, drain)


def hand_over(src, dst, held, in_sem, out_sem):
    size = src.shape[0] // PIECES
    at = [pl.ds(i * size, size) for i in range(PIECES)]
    loads = [pltpu.make_async_copy(src.at[a], held.at[a], in_sem.at[i]) for i, a in enumerate(at)]
    saves = [pltpu.make_async_copy(held.at[a], dst.at[a], out_sem.at[i]) for i, a in enumerate(at)]
    for c in loads:
        c.start()
    for c, d in zip(loads, saves):
        c.wait()
        d.start()
    for d in saves:
        d.wait()


def shards(activations, gate_values, accepted, seg_starts, mr_taps, lr_rate, lr_angle, lr_residue):
    rows, width = activations.shape
    count, taps = mr_taps.shape
    modes = lr_rate.shape[1]
    n = lax.axis_size("seq")
    teams = n // TEAM
    span = width // CHUNKS
    quarter = span // TEAM
    tiles = span // LANES
    both = 2 * modes

    def dma(*shape):
        return pltpu.SemaphoreType.DMA(shape)

    hbm = pl.BlockSpec(memory_space=pltpu.HBM)
    mask = pltpu.VMEM((rows, LANES), bf16)
    part, part32 = pltpu.VMEM((CHUNKS, both, quarter), bf16), pltpu.VMEM((CHUNKS, both, quarter), f32)
    four = pltpu.VMEM((CHUNKS, 2, 2, both, quarter), bf16)
    gated = pl.pallas_call(
        functools.partial(kernel, n),
        in_specs=[hbm] * 8,
        out_specs=hbm,
        out_shape=jax.ShapeDtypeStruct((rows, width), bf16),
        scratch_shapes=[
            pltpu.VMEM((1, rows), jnp.int32), pltpu.VMEM((1, rows), jnp.int32), pltpu.VMEM((count, taps), bf16),
            pltpu.VMEM((modes, count), f32), pltpu.VMEM((modes, count), f32), pltpu.VMEM((2, modes, count), f32),
            pltpu.VMEM((rows, width), bf16), pltpu.VMEM((2, rows, width), bf16),
            pltpu.VMEM((rows, width), bf16), pltpu.VMEM((rows, width), bf16),
            pltpu.VMEM((count, taps), f32), pltpu.VMEM((rows, width), f32),
            pltpu.VMEM((count, taps), f32), pltpu.VMEM((width // LANES * 8, LANES), f32),
            pltpu.VMEM((4, modes, count), f32), pltpu.VMEM((both, count), f32),
            pltpu.VMEM((tiles, 8 * rows, 2 * rows), bf16), pltpu.VMEM((tiles, 4 * rows, 2 * rows), bf16),
            mask, mask, mask, mask, mask,
            pltpu.VMEM((16, LANES), f32), pltpu.VMEM((TEAM, 16, LANES), f32), pltpu.VMEM((16, LANES), f32),
            pltpu.VMEM((8, LANES), f32), pltpu.VMEM((teams, 8, LANES), f32),
            four, four, part32, part, part, part32,
            part, pltpu.VMEM((CHUNKS, teams, both, quarter), bf16), part32, part, part,
            pltpu.VMEM((CHUNKS, 2, both, quarter), bf16), four,
            pltpu.VMEM((rows, width), bf16),
            dma(6), dma(3, CHUNKS), dma(CHUNKS), dma(CHUNKS), dma(CHUNKS), dma(TEAM), dma(TEAM), dma(1), dma(1), dma(teams), dma(teams),
            dma(CHUNKS), dma(CHUNKS), dma(CHUNKS), dma(CHUNKS), dma(CHUNKS, teams), dma(CHUNKS, teams),
            dma(CHUNKS), dma(CHUNKS), dma(CHUNKS), dma(CHUNKS)],
        compiler_params=pltpu.CompilerParams(collective_id=0, has_side_effects=True,
                                             vmem_limit_bytes=54 * 2**20),
        name="hyena",
    )(activations, gate_values, accepted[None, :], seg_starts[None, :], mr_taps, lr_rate.T, lr_angle.T,
      jnp.swapaxes(lr_residue, 1, 2))
    return pl.pallas_call(
        hand_over,
        in_specs=[hbm],
        out_specs=hbm,
        out_shape=jax.ShapeDtypeStruct((rows, width), bf16),
        scratch_shapes=[pltpu.VMEM((rows, width), bf16), dma(PIECES), dma(PIECES)],
        compiler_params=pltpu.CompilerParams(vmem_limit_bytes=58 * 2**20),
        name="hand_over",
    )(gated)


def solution(mesh):
    return jax.shard_map(
        shards,
        mesh=mesh,
        in_specs=(P(("groups", "seq"), None), P(None, ("groups", "seq"), None), P(("groups", "seq")),
                  P(("groups", "seq")), P(), P(), P(), P()),
        out_specs=P(("groups", "seq"), None),
        check_vma=False,
    )
```
